32 devices in a mesh: stream: 8 (over y, x, core), wall: 4 (over z).
Axes of the slice: x: 2, y: 2, z: 4, core: 2. Of those that a mesh axis runs over, the one named last changes fastest.
Arguments:
- velocity: float32 [3, 2, 768, 2048], P(None, None, 'wall', 'stream'), may hold values from -96 to 96
- viscosity: float32 [2, 768, 2048], P(None, 'wall', 'stream'), may hold values from 2 to 4000000
- y_coef: float32 [2, 768], P(None, 'wall'), may hold values from 0.05 to 0.25
Outputs:
- updated: float32 [3, 2, 768, 2048], P(None, None, 'wall', 'stream')
The draws below stay inside these ranges and needn't reach their ends.
All inputs are finite; a program needn't handle non-finite values.
Results may differ from the reference program's by a relative error of at most 0.0015.
Values sent between devices are 32-bit elements; how exact they have to be, the bound alone decides.
A program may use at most 64 MiB of HBM per device.

```python
import math
import jax
import jax.numpy as jnp
from jax import lax

COMPONENTS = 3
PLANES = 2
NX = 2048
NY = 768


def draw_viscosity(key, part):
    line_key = jax.random.fold_in(key, 11)
    cell_key = jax.random.fold_in(key, 23)
    line_low = math.log(4.0)
    cell_half = math.log(2.0)
    line_high = math.log(1000000.0)
    line_log = jax.random.uniform(line_key, (PLANES, NY, 1), jnp.float32, line_low, line_high)
    cell_log = jax.random.uniform(cell_key, (PLANES, NY, NX), jnp.float32, -cell_half, cell_half)
    return jnp.exp(line_log + cell_log).astype(jnp.float32)


def steps_of(key, dims, split, smallest, high):
    def one(position, parts):
        heights = jax.random.uniform(jax.random.fold_in(jax.random.fold_in(key, 6), position), (parts,), jnp.float32, smallest / len(split), high / len(split))
        return jnp.repeat(jnp.exp(heights), dims[position] // parts).reshape((-1,) + (1,) * (len(dims) - position - 1))

    gain = one(*split[0])
    for cut in split[1:]:
        gain = gain * one(*cut)
    return gain


def centred(rng, extent, scale, limit, pieces=(), held_as=jnp.bfloat16):
    level = steps_of(rng, extent, pieces, -0.22, 0.18) if pieces else 1.0
    values = jax.random.normal(rng, extent, jnp.float32) * scale * level
    return jnp.minimum(jnp.maximum(values, -limit), limit).astype(held_as)


def setup_inputs(seed: int = 0) -> dict:
    streams_of = jax.random.split(jax.random.key(seed), 4)
    velocity = centred(streams_of[0], (COMPONENTS, PLANES, NY, NX), 16.0, 96.0, ((2, 4), (3, 8)), jnp.float32)
    viscosity = draw_viscosity(jax.random.fold_in(streams_of[3], 71), 0)
    y_coef = jnp.clip(jnp.exp(math.log(0.25) - 1.609438 * jax.random.uniform(streams_of[2], (2, NY), jnp.float32) ** steps_of(streams_of[2], (2, NY), ((1, 4),), -0.2, 0.2)), 0.05, 0.25)
    return {"velocity": velocity, "viscosity": viscosity, "y_coef": y_coef}


def thomas_sweep(lower_t, diag_t, upper_t, source_t):
    def forward(carry, entry):
        ratio_prev, value_prev = carry
        low_e, dia_e, upp_e, src_e = entry
        denom = dia_e - low_e * ratio_prev
        ratio_new = upp_e / denom
        value_new = (src_e - low_e[None] * value_prev) / denom[None]
        return (ratio_new, value_new), (ratio_new, value_new)

    start = (jnp.zeros_like(diag_t[0]), jnp.zeros_like(source_t[0]))
    _, (ratios, values) = lax.scan(forward, start, (lower_t, diag_t, upper_t, source_t))

    def backward(following, entry):
        ratio_e, value_e = entry
        current = value_e - ratio_e[None] * following
        return current, current

    _, solved = lax.scan(backward, jnp.zeros_like(source_t[0]), (ratios, values), reverse=True)
    return solved


def solve_plane(inputs):
    lower_p, diag_p, upper_p, source_p = inputs
    lower_t = lower_p.T
    diag_t = diag_p.T
    upper_t = upper_p.T
    source_t = jnp.transpose(source_p, (2, 0, 1))
    gamma = -diag_t[0]
    last_diag = diag_t[-1] - lower_t[0] * upper_t[-1] / gamma
    diag_mod = jnp.concatenate([(diag_t[0] - gamma)[None], diag_t[1:-1], last_diag[None]], axis=0)
    lower_mod = jnp.concatenate([jnp.zeros_like(lower_t[:1]), lower_t[1:]], axis=0)
    middle = jnp.zeros_like(diag_t[1:-1])
    spike = jnp.concatenate([gamma[None], middle, upper_t[-1][None]], axis=0)[:, None, :]
    solved = thomas_sweep(lower_mod, diag_mod, upper_t, jnp.concatenate([source_t, spike], axis=1))
    plain = solved[:, :3]
    spiked = solved[:, 3:]
    factor = (lower_t[0] / gamma)
    plain_dot = plain[0] + factor[None] * plain[-1]
    spiked_dot = spiked[0] + factor[None] * spiked[-1]
    result = plain - spiked * (plain_dot / (1.0 + spiked_dot))[None]
    return jnp.transpose(result, (1, 2, 0))


def reference(velocity, viscosity, y_coef):
    padded = jnp.pad(velocity, ((0, 0), (0, 0), (1, 1), (0, 0)))
    coef_up = y_coef[0][None, None, :, None]
    coef_down = y_coef[1][None, None, :, None]
    source = velocity + coef_up * (padded[:, :, 2:] - velocity) - coef_down * (velocity - padded[:, :, :-2])
    stiffness = viscosity
    lower = -0.5 * (jnp.roll(stiffness, 1, axis=-1) + stiffness)
    upper = -0.5 * (stiffness + jnp.roll(stiffness, -1, axis=-1))
    diagonal = 1.0 - lower - upper
    planes_out = lax.map(solve_plane, (lower, diagonal, upper, jnp.transpose(source, (1, 0, 2, 3))))
    return jnp.transpose(planes_out, (1, 0, 2, 3))
```

```python
import functools

import jax
import jax.numpy as jnp
from jax import lax
from jax.experimental import pallas as pl
from jax.experimental.pallas import tpu as pltpu
from jax.sharding import PartitionSpec as P

SEGMENTS = 8
PIECES = 4
LANES = 128
MESH = pl.DeviceIdType.MESH


def up8(rows):
    return -(-rows // 8) * 8


def join_matrix(a, b, link):
    a00, a0l, all_ = a
    b00, b0l, bll = b
    gain = link / (1.0 + link * (all_ + b00))
    left = gain * a0l
    right = gain * b0l
    return (a00 - left * a0l, left * b0l, bll - right * b0l), (gain, left, right)


def join_values(a, b, weights):
    _, left, right = weights
    jump = [al - b0 for al, b0 in zip(a[1], b[0])]
    first = [a0 - left * j for a0, j in zip(a[0], jump)]
    last = [bl + right * j for bl, j in zip(b[1], jump)]
    return (first, last), jump


def join_tree(blocks):
    levels = []
    while len(blocks) > 1:
        merged, weights = [], []
        for i in range(0, len(blocks) - 1, 2):
            (ma, fa, la), (mb, fb, lb) = blocks[i], blocks[i + 1]
            m, w = join_matrix(ma, mb, 0.5 * (la + fb))
            merged.append((m, fa, lb))
            weights.append(w)
        if len(blocks) % 2:
            merged.append(blocks[-1])
        levels.append(weights)
        blocks = merged
    return blocks[0], levels


def value_tree(values, levels):
    jumps = []
    for weights in levels:
        merged, jump = [], []
        for i, w in enumerate(weights):
            v, j = join_values(values[2 * i], values[2 * i + 1], w)
            merged.append(v)
            jump.append(j)
        if len(values) % 2:
            merged.append(values[-1])
        jumps.append(jump)
        values = merged
    return values[0], jumps


def down_tree(levels, jumps, inflow, outflow):
    flows = [(inflow, outflow)]
    for depth in reversed(range(len(levels))):
        spread = []
        for i, (gain, left, right) in enumerate(levels[depth]):
            fin, fout = flows[i]
            middle = None
            for term, weight in ((fin, left), (fout, right)):
                if term is not None:
                    part = weight if isinstance(term, float) else term * weight
                    middle = part if middle is None else middle + part
            if jumps is not None:
                part = gain * jumps[depth][i]
                middle = part if middle is None else middle + part
            spread += [(fin, middle), (middle, fout)]
        flows = spread + flows[len(levels[depth]) :]
    return flows


def odd(rows):
    return rows | 1


def total(terms):
    result = None
    for term in terms:
        if term is not None:
            result = term if result is None else result + term
    return result


def times(weight, flow):
    return None if flow is None else weight if isinstance(flow, float) else weight * flow


def kernel(devices, wall_devices, planes, vel_hbm, visc_hbm, coef_hbm, out,
           vel, visc, coef, edge, wall_out, got_w, stiff_t, src, src_t, ratio_s, inv_s, head_s, y_s, seg_a, seg_b,
           seg_f, flow, sol_t, sol, rim, rim_t, rim_sol, weigh, coef_s, msg_a, msg_b, msg_c, got_a, got_b, got_c,
           load_sem, edge_sem, wall_send, wall_recv, a_send, a_recv, b_send, b_recv, c_send, c_recv):
    slabs, rows, cells = vel_hbm.shape
    components = slabs // planes
    lines = planes * rows
    groups = lines // LANES
    length = cells // SEGMENTS
    piece = length // PIECES
    pitch = odd(length)
    step = odd(groups)
    me = lax.axis_index("stream")
    wall = lax.axis_index("wall")
    has_below = wall > 0
    has_above = wall < wall_devices - 1
    barrier = pltpu.get_barrier_semaphore()
    edges = [
        pltpu.make_async_copy(vel_hbm.at[:, rows - 8 : rows, :], edge.at[0], edge_sem.at[0]),
        pltpu.make_async_copy(vel_hbm.at[:, 0:8, :], edge.at[1], edge_sem.at[1]),
    ]
    loads = [
        pltpu.make_async_copy(visc_hbm, visc, load_sem.at[0]),
        pltpu.make_async_copy(coef_hbm, coef, load_sem.at[1]),
        pltpu.make_async_copy(vel_hbm, vel.at[:, 8 : 8 + rows, :], load_sem.at[2]),
    ]
    for load in edges + loads:
        load.start()

    def around(d):
        return lax.rem(me + d, devices)

    def greet(target):
        for d in range(devices):
            pl.semaphore_signal(
                barrier, inc=1, device_id={"wall": target, "stream": around(d)}, device_id_type=MESH)

    @pl.when(has_below)
    def _():
        greet(wall - 1)

    @pl.when(has_above)
    def _():
        greet(wall + 1)

    for d in range(1, devices):
        pl.semaphore_signal(barrier, inc=1, device_id={"stream": around(d)}, device_id_type=MESH)

    nothing = jnp.zeros((slabs, 1, cells), jnp.float32)
    vel[:, 7:8, :] = nothing
    vel[:, 8 + rows : 9 + rows, :] = nothing
    wall_out[...] = jnp.zeros(wall_out.shape, jnp.float32)
    for load in edges:
        load.wait()
    for a in range(slabs):
        wall_out[0, a : a + 1, :] = edge[0, a, 7:8, :]
        wall_out[1, a : a + 1, :] = edge[1, a, 0:1, :]

    def wall_copy(side, d, target):
        return pltpu.make_async_remote_copy(
            src_ref=wall_out.at[side], dst_ref=got_w.at[side, d],
            send_sem=wall_send.at[side, d], recv_sem=wall_recv.at[side, d],
            device_id={"wall": target, "stream": around(d)}, device_id_type=MESH)

    def ring_copy(d, source, target, send, recv):
        return pltpu.make_async_remote_copy(
            src_ref=source, dst_ref=target.at[d - 1],
            send_sem=send.at[d - 1], recv_sem=recv.at[d - 1],
            device_id={"stream": around(d)}, device_id_type=MESH)

    def at_position(i):
        return pl.ds(i, SEGMENTS, stride=pitch)

    def put_segments(buffer, slot, value):
        for g in range(groups):
            buffer[slot, pl.ds(g, SEGMENTS, stride=step), :] = value[g]

    def take_segment(buffer, slot, s):
        return buffer[slot, s * step : s * step + groups, :]

    def spread_rows(target, turned):
        for s in range(SEGMENTS):
            target[s * pitch : s * pitch + length, :] = turned[s * length : (s + 1) * length, :]

    def gather_rows(source):
        return jnp.concatenate([source[s * pitch : s * pitch + length, :] for s in range(SEGMENTS)])

    def factor(source, g):
        one = jnp.ones((SEGMENTS, LANES), jnp.float32)
        excess, reach = [one] * PIECES, [one] * PIECES
        corner = [None] * PIECES
        stiff = [source[at_position(b * piece), :] for b in range(PIECES)]
        starts = list(stiff)
        blocks = []
        for t in range(piece):
            for b in range(PIECES):
                i = b * piece + t
                if t < piece - 1:
                    following = source[at_position(i + 1), :]
                    link = 0.5 * (stiff[b] + following)
                    stiff[b] = following
                    inv = 1.0 / (excess[b] + link)
                    ratio = link * inv
                    ratio_s[i, g] = ratio
                else:
                    inv = 1.0 / excess[b]
                head = reach[b] * inv
                inv_s[i, g] = inv
                head_s[i, g] = head
                corner[b] = head * reach[b] if t == 0 else corner[b] + head * reach[b]
                if t < piece - 1:
                    excess[b] = 1.0 + ratio * excess[b]
                    reach[b] = reach[b] * ratio
                else:
                    blocks.append(((corner[b], head, inv), starts[b], stiff[b]))
        return blocks

    def forward(load, keep, g, fields):
        y = [[None] * fields for _ in range(PIECES)]
        first = [[None] * fields for _ in range(PIECES)]
        final = [[None] * fields for _ in range(PIECES)]
        for t in range(piece):
            for b in range(PIECES):
                i = b * piece + t
                head = head_s[i, g]
                ratio = ratio_s[i - 1, g] if t else None
                for c in range(fields):
                    f = load(c, i)
                    y[b][c] = f + ratio * y[b][c] if t else f
                    keep(c, i, y[b][c])
                    first[b][c] = first[b][c] + head * y[b][c] if t else head * y[b][c]
                    if t == piece - 1:
                        final[b][c] = inv_s[i, g] * y[b][c]
        return first, final

    def backward(spread, kept, put, g):
        for b in range(PIECES):
            now = [None] * len(spread)
            for t in reversed(range(piece)):
                i = b * piece + t
                head = head_s[i, g]
                inv = inv_s[i, g]
                if t < piece - 1:
                    ratio = ratio_s[i, g]
                for f in range(len(spread)):
                    fin, fout = spread[f][b]
                    terms = [times(head, fin)]
                    if kept is not None:
                        terms.append(kept(f, i) * inv)
                    if t < piece - 1:
                        terms.append(ratio * now[f])
                    value = total(terms)
                    if t == piece - 1 and fout is not None:
                        value = value - fout * inv
                    now[f] = value
                    put(f, i, value)

    loads[0].wait()
    parts = []
    for g in range(groups):
        spread_rows(stiff_t.at[g], visc[g * LANES : (g + 1) * LANES, :].T)
        parts.append(factor(stiff_t.at[g], g))
    blocks = [
        (tuple(jnp.stack([p[b][0][q] for p in parts]) for q in range(3)),
         jnp.stack([p[b][1] for p in parts]), jnp.stack([p[b][2] for p in parts]))
        for b in range(PIECES)
    ]
    whole, piece_levels = join_tree(blocks)
    for slot, value in enumerate(whole[0] + whole[1:]):
        put_segments(seg_a, slot, value)
    blocks = []
    for s in range(SEGMENTS):
        v = [take_segment(seg_a, slot, s) for slot in range(5)]
        blocks.append((tuple(v[:3]), v[3], v[4]))
    mine, levels = join_tree(blocks)
    for q, value in enumerate(mine[0] + (mine[1], mine[2])):
        msg_a[q * groups : (q + 1) * groups, :] = value

    beside = jnp.where(has_below, devices, 0) + jnp.where(has_above, devices, 0)
    pl.semaphore_wait(barrier, devices - 1 + beside)

    @pl.when(has_above)
    def _():
        for d in range(devices):
            wall_copy(0, d, wall + 1).start()

    @pl.when(has_below)
    def _():
        for d in range(devices):
            wall_copy(1, d, wall - 1).start()

    @pl.when(jnp.logical_not(has_below))
    def _():
        got_w[0] = jnp.zeros(got_w.shape[1:], jnp.float32)

    @pl.when(jnp.logical_not(has_above))
    def _():
        got_w[1] = jnp.zeros(got_w.shape[1:], jnp.float32)

    for d in range(1, devices):
        ring_copy(d, msg_a, got_a, a_send, a_recv).start()
    loads[1].wait()
    coef_s[...] = jnp.zeros(coef_s.shape, jnp.float32)
    coef_s[0:2, 0:rows] = coef[...]
    slopes = coef_s[...].T
    loads[2].wait()
    for r in range(0, rows, 8):
        up = jnp.broadcast_to(slopes[r : r + 8, 0:1], (8, LANES))
        down = jnp.broadcast_to(slopes[r : r + 8, 1:2], (8, LANES))
        keep = 1.0 - up - down
        for a in range(slabs):
            c, p = a // planes, a % planes
            for h in range(0, cells, LANES):
                lane = slice(h, h + LANES)
                src[c, p * rows + r : p * rows + r + 8, lane] = (
                    keep * vel[a, 8 + r : 16 + r, lane]
                    + up * vel[a, 9 + r : 17 + r, lane]
                    + down * vel[a, 7 + r : 15 + r, lane]
                )
    firsts, finals = [], []
    for g in range(groups):
        for c in range(components):
            spread_rows(src_t.at[c, g], src[c, g * LANES : (g + 1) * LANES, :].T)

        def keep_y(c, i, value, g=g):
            y_s[c, i, g] = value

        first, final = forward(lambda c, i, g=g: src_t[c, g, at_position(i), :], keep_y, g, components)
        firsts.append(first)
        finals.append(final)
    values = [
        ([jnp.stack([v[b][c] for v in firsts]) for c in range(components)],
         [jnp.stack([v[b][c] for v in finals]) for c in range(components)])
        for b in range(PIECES)
    ]
    whole, piece_jumps = value_tree(values, piece_levels)
    for slot, value in enumerate(whole[0] + whole[1]):
        put_segments(seg_b, slot, value)
    values = []
    for s in range(SEGMENTS):
        v = [take_segment(seg_b, slot, s) for slot in range(2 * components)]
        values.append((v[:components], v[components:]))
    own, jumps = value_tree(values, levels)
    for q, value in enumerate(own[0] + own[1]):
        msg_b[q * groups : (q + 1) * groups, :] = value
    for d in range(1, devices):
        ring_copy(d, msg_b, got_b, b_send, b_recv).start()
    zero = jnp.zeros((groups, LANES), jnp.float32)
    unit = jnp.ones((groups, LANES), jnp.float32)

    def solve_fields(chosen):
        for f in chosen:
            if f < components:
                picked = [[j[f] for j in level] for level in jumps]
                flows = down_tree(levels, picked, None, None)
            elif f == components:
                flows = down_tree(levels, None, 1.0, None)
            else:
                flows = down_tree(levels, None, None, 1.0)
            for s, (fin, fout) in enumerate(flows):
                for side, term in enumerate((fin, fout)):
                    term = zero if term is None else unit if isinstance(term, float) else term
                    seg_f[2 * f + side, s * step : s * step + groups, :] = term
        for g in range(groups):
            near = [[tuple(w[g] for w in weights) for weights in level] for level in piece_levels]
            spread = []
            for f in chosen:
                fin, fout = (seg_f[2 * f + side, pl.ds(g, SEGMENTS, stride=step), :] for side in range(2))
                picked = [[j[f][g] for j in level] for level in piece_jumps] if f < components else None
                spread.append(down_tree(near, picked, fin, fout))

            def put(n, i, value, g=g):
                sol_t[chosen[n], g, at_position(i), :] = value

            kept = None if chosen[0] >= components else lambda n, i, g=g: y_s[chosen[n], i, g]
            backward(spread, kept, put, g)
            for f in chosen:
                sol[f, g * LANES : (g + 1) * LANES, :] = gather_rows(sol_t.at[f, g]).T

    solve_fields([components, components + 1])
    ends = [(side, p, p * rows + side * (rows - 1)) for side in range(2) for p in range(planes)]
    for side, p, r in ends:
        for f in range(2):
            e = (f * 2 + side) * planes + p
            msg_c[e : e + 1, :] = sol[components + f, r : r + 1, :]
    for d in range(1, devices):
        ring_copy(d, msg_c, got_c, c_send, c_recv).start()
    solve_fields(list(range(components)))
    rim[...] = jnp.ones(rim.shape, jnp.float32)
    for side, p, r in ends:
        for c in range(components):
            e = side * 8 + c * planes + p
            rim[e : e + 1, :] = visc[r : r + 1, :]
    spread_rows(rim_t.at[0], rim[...].T)
    whole, rim_piece_levels = join_tree(factor(rim_t.at[0], groups))
    rim_blocks = whole[0] + whole[1:]
    for slot, value in enumerate(rim_blocks):
        seg_a[slot, 0:SEGMENTS, :] = value
    blocks = []
    for s in range(SEGMENTS):
        v = [seg_a[slot, s : s + 1, :] for slot in range(5)]
        blocks.append((tuple(v[:3]), v[3], v[4]))
    _, rim_levels = join_tree(blocks)

    @pl.when(has_below)
    def _():
        wall_copy(0, 0, wall).wait_recv()

    @pl.when(has_above)
    def _():
        wall_copy(1, 0, wall).wait_recv()

    scales = (slopes[0:1, 1:2], slopes[rows - 1 : rows, 0:1])
    for side in range(2):
        rim[side * 8 : side * 8 + 8, :] = got_w[side, 0] * scales[side]
    spread_rows(rim_t.at[0], rim[...].T)
    held = {}

    def keep_rim(c, i, value):
        held[i] = value

    first, final = forward(lambda c, i: rim_t[0, at_position(i), :], keep_rim, groups, 1)
    whole, rim_piece_jumps = value_tree([(first[b], final[b]) for b in range(PIECES)], rim_piece_levels)
    seg_b[0, 0:SEGMENTS, :] = whole[0][0]
    seg_b[1, 0:SEGMENTS, :] = whole[1][0]
    _, rim_jumps = value_tree(
        [([seg_b[0, s : s + 1, :]], [seg_b[1, s : s + 1, :]]) for s in range(SEGMENTS)], rim_levels)
    picked = [[j[0] for j in level] for level in rim_jumps]
    for s, terms in enumerate(down_tree(rim_levels, picked, None, None)):
        for side, term in enumerate(terms):
            term = jnp.zeros((1, LANES), jnp.float32) if term is None else term
            seg_f[side, s : s + 1, :] = term
    picked = [[j[0] for j in level] for level in rim_piece_jumps]
    spread = [down_tree(rim_piece_levels, picked, seg_f[0, 0:SEGMENTS, :], seg_f[1, 0:SEGMENTS, :])]

    def put_rim(n, i, value):
        rim_t[1, at_position(i), :] = value

    backward(spread, lambda n, i: held[i], put_rim, groups)
    rim_sol[...] = gather_rows(rim_t.at[1]).T
    for d in range(1, devices):
        ring_copy(d, msg_a, got_a, a_send, a_recv).wait()
    others = []
    for t in range(1, devices):
        slot = devices - t - 1
        v = [got_a[slot, q * groups : (q + 1) * groups, :] for q in range(5)]
        others.append((tuple(v[:3]), v[3], v[4]))
    rest, ring_levels = join_tree(others)
    (m00, m0l, mll), m_first, m_last = mine
    (b00, b0l, bll), b_first, b_last = rest
    out_diag = 2.0 / (m_last + b_first) + mll + b00
    in_diag = 2.0 / (b_last + m_first) + bll + m00
    cross = m0l + b0l
    det = 1.0 / (out_diag * in_diag - cross * cross)
    near_in, near_out, across = out_diag * det, in_diag * det, cross * det

    def put_weights(d, weights):
        for n, value in enumerate(weights):
            for g in range(groups):
                k = 4 * d + n
                weigh[g, k : k + 1, :] = value[g : g + 1]

    put_weights(0, (0.0 - near_in, 0.0 - across, 0.0 - across, 0.0 - near_out))
    to_first = down_tree(ring_levels, None, 1.0, None)
    to_last = down_tree(ring_levels, None, None, 1.0)
    for t in range(1, devices):
        pairs = list(zip(to_first[t - 1], to_last[t - 1]))
        weights = []
        for by_first, by_last in ((across, near_in), (near_out, across)):
            for from_first, from_last in pairs:
                weights.append(0.0 - total((times(by_first, from_first), times(by_last, from_last))))
        put_weights(devices - t, weights)
    row_plane = lax.broadcasted_iota(jnp.int32, (8, 1), 0) % planes

    def by_plane(pick):
        tile = pick(0)
        for p in range(1, planes):
            tile = jnp.where(row_plane == p, pick(p), tile)
        return tile

    turned = [weigh[g].T for g in range(groups)]
    tables = []
    for side in range(2):
        def pick(p):
            r = p * rows + side * (rows - 1)
            line = r % LANES
            return turned[r // LANES][line : line + 1, :]
        tables.append(by_plane(pick) * scales[side])
    for d in range(1, devices):
        ring_copy(d, msg_b, got_b, b_send, b_recv).wait()
    theirs = []
    for t in range(1, devices):
        slot = devices - t - 1
        v = [got_b[slot, q * groups : (q + 1) * groups, :] for q in range(2 * components)]
        theirs.append((v[:components], v[components:]))
    tail, _ = value_tree(theirs, ring_levels)
    for c in range(components):
        gap_out = own[1][c] - tail[0][c]
        gap_in = tail[1][c] - own[0][c]
        outflow = near_out * gap_out + across * gap_in
        inflow = near_in * gap_in + across * gap_out
        for g in range(groups):
            flow[g, c : c + 1, :] = inflow[g : g + 1]
            flow[g, components + c : components + c + 1, :] = outflow[g : g + 1]

    for g in range(groups):
        span = slice(g * LANES, (g + 1) * LANES)
        columns = flow[g].T
        from_left = sol[components, span, :]
        from_right = sol[components + 1, span, :]
        for c in range(components):
            out[c, span, :] = (
                sol[c, span, :]
                + columns[:, c : c + 1] * from_left
                + columns[:, components + c : components + c + 1] * from_right
            )
    for d in range(1, devices):
        ring_copy(d, msg_c, got_c, c_send, c_recv).wait()

    def side_rows(d, f, side):
        source = msg_c if d == 0 else got_c.at[d - 1]
        base = (f * 2 + side) * planes
        return by_plane(lambda p: source[base + p : base + p + 1, :])

    weights = {}
    for side in range(2):
        for d in range(devices):
            left, right = side_rows(d, 0, side), side_rows(d, 1, side)
            for way in range(2):
                k = 4 * d + 2 * way
                weights[side, d, way] = tables[side][:, k : k + 1] * left + tables[side][:, k + 1 : k + 2] * right

    @pl.when(has_below)
    def _():
        for d in range(1, devices):
            wall_copy(0, d, wall).wait_recv()

    @pl.when(has_above)
    def _():
        for d in range(1, devices):
            wall_copy(1, d, wall).wait_recv()

    for side in range(2):
        ways = []
        for way in range(2):
            sums = total([got_w[side, d] * weights[side, d, way] for d in range(devices)])
            ways.append(jnp.sum(sums, axis=1, keepdims=True))
        added = (
            rim_sol[side * 8 : side * 8 + 8, :] + ways[0] * side_rows(0, 0, side) + ways[1] * side_rows(0, 1, side)
        )
        for c in range(components):
            for p in range(planes):
                r = p * rows + side * (rows - 1)
                e = c * planes + p
                out[c, r : r + 1, :] = out[c, r : r + 1, :] + added[e : e + 1, :]

    @pl.when(has_above)
    def _():
        for d in range(devices):
            wall_copy(0, d, wall + 1).wait_send()

    @pl.when(has_below)
    def _():
        for d in range(devices):
            wall_copy(1, d, wall - 1).wait_send()


def shards(devices, wall_devices, velocity, viscosity, y_coef):
    components, planes, rows, cells = velocity.shape
    lines = planes * rows
    slabs = components * planes
    groups = lines // LANES
    length = cells // SEGMENTS
    fields = components + 2
    f32 = jnp.float32
    rows_a, rows_b, rows_c = up8(5 * groups), up8(2 * components * groups), up8(4 * planes)
    peers = devices - 1
    sweeps = (length, groups + 1, SEGMENTS, LANES)
    turned = (SEGMENTS * odd(length), LANES)
    joints = SEGMENTS * odd(groups)
    vmem = pl.BlockSpec(memory_space=pltpu.VMEM)
    result = pl.pallas_call(
        functools.partial(kernel, devices, wall_devices, planes),
        out_shape=jax.ShapeDtypeStruct((components, lines, cells), f32),
        in_specs=[pl.BlockSpec(memory_space=pltpu.HBM)] * 3,
        out_specs=vmem,
        scratch_shapes=[
            pltpu.VMEM((slabs, rows + 16, cells), f32),
            pltpu.VMEM((lines, cells), f32),
            pltpu.VMEM(y_coef.shape, f32),
            pltpu.VMEM((2, slabs, 8, cells), f32),
            pltpu.VMEM((2, 8, cells), f32),
            pltpu.VMEM((2, devices, 8, cells), f32),
            pltpu.VMEM((groups,) + turned, f32),
            pltpu.VMEM((components, lines, cells), f32),
            pltpu.VMEM((components, groups) + turned, f32),
            pltpu.VMEM(sweeps, f32),
            pltpu.VMEM(sweeps, f32),
            pltpu.VMEM(sweeps, f32),
            pltpu.VMEM((components, length, groups, SEGMENTS, LANES), f32),
            pltpu.VMEM((5, joints, LANES), f32),
            pltpu.VMEM((2 * components, joints, LANES), f32),
            pltpu.VMEM((2 * fields, joints, LANES), f32),
            pltpu.VMEM((groups, up8(2 * components), LANES), f32),
            pltpu.VMEM((fields, groups) + turned, f32),
            pltpu.VMEM((fields, lines, cells), f32),
            pltpu.VMEM((LANES, cells), f32),
            pltpu.VMEM((2,) + turned, f32),
            pltpu.VMEM((LANES, cells), f32),
            pltpu.VMEM((groups, 4 * devices, LANES), f32),
            pltpu.VMEM((8, -(-rows // LANES) * LANES), f32),
            pltpu.VMEM((rows_a, LANES), f32),
            pltpu.VMEM((rows_b, LANES), f32),
            pltpu.VMEM((rows_c, cells), f32),
            pltpu.VMEM((peers, rows_a, LANES), f32),
            pltpu.VMEM((peers, rows_b, LANES), f32),
            pltpu.VMEM((peers, rows_c, cells), f32),
            pltpu.SemaphoreType.DMA((3,)),
            pltpu.SemaphoreType.DMA((2,)),
            pltpu.SemaphoreType.DMA((2, devices)),
            pltpu.SemaphoreType.DMA((2, devices)),
        ] + [pltpu.SemaphoreType.DMA((peers,))] * 6,
        compiler_params=pltpu.CompilerParams(
            collective_id=0, has_side_effects=True, vmem_limit_bytes=40 * 1024 * 1024
        ),
        name="implicit_lines",
    )(
        pltpu.with_memory_space_constraint(velocity.reshape(slabs, rows, cells), pltpu.HBM),
        pltpu.with_memory_space_constraint(viscosity.reshape(lines, cells), pltpu.HBM),
        pltpu.with_memory_space_constraint(y_coef, pltpu.HBM),
    )
    return result.reshape(velocity.shape)


def solution(mesh):
    placed = (P(None, None, "wall", "stream"), P(None, "wall", "stream"), P(None, "wall"))
    return jax.shard_map(
        functools.partial(shards, mesh.shape["stream"], mesh.shape["wall"]),
        mesh=mesh,
        in_specs=placed,
        out_specs=P(None, None, "wall", "stream"),
        check_vma=False,
    )
```

```python
import functools

import jax
import jax.numpy as jnp
from jax import lax
from jax.experimental import pallas as pl
from jax.experimental.pallas import tpu as pltpu
from jax.sharding import PartitionSpec as P

SEGMENTS = 8
PIECES = 4
LANES = 128
MESH = pl.DeviceIdType.MESH


def up8(rows):
    return -(-rows // 8) * 8


def join_matrix(a, b, link):
    a00, a0l, all_ = a
    b00, b0l, bll = b
    gain = link / (1.0 + link * (all_ + b00))
    left = gain * a0l
    right = gain * b0l
    return (a00 - left * a0l, left * b0l, bll - right * b0l), (gain, left, right)


def join_values(a, b, weights):
    _, left, right = weights
    jump = [al - b0 for al, b0 in zip(a[1], b[0])]
    first = [a0 - left * j for a0, j in zip(a[0], jump)]
    last = [bl + right * j for bl, j in zip(b[1], jump)]
    return (first, last), jump


def join_tree(blocks):
    levels = []
    while len(blocks) > 1:
        merged, weights = [], []
        for i in range(0, len(blocks) - 1, 2):
            (ma, fa, la), (mb, fb, lb) = blocks[i], blocks[i + 1]
            m, w = join_matrix(ma, mb, 0.5 * (la + fb))
            merged.append((m, fa, lb))
            weights.append(w)
        if len(blocks) % 2:
            merged.append(blocks[-1])
        levels.append(weights)
        blocks = merged
    return blocks[0], levels


def value_tree(values, levels):
    jumps = []
    for weights in levels:
        merged, jump = [], []
        for i, w in enumerate(weights):
            v, j = join_values(values[2 * i], values[2 * i + 1], w)
            merged.append(v)
            jump.append(j)
        if len(values) % 2:
            merged.append(values[-1])
        jumps.append(jump)
        values = merged
    return values[0], jumps


def down_tree(levels, jumps, inflow, outflow):
    flows = [(inflow, outflow)]
    for depth in reversed(range(len(levels))):
        spread = []
        for i, (gain, left, right) in enumerate(levels[depth]):
            fin, fout = flows[i]
            middle = None
            for term, weight in ((fin, left), (fout, right)):
                if term is not None:
                    part = weight if isinstance(term, float) else term * weight
                    middle = part if middle is None else middle + part
            if jumps is not None:
                part = gain * jumps[depth][i]
                middle = part if middle is None else middle + part
            spread += [(fin, middle), (middle, fout)]
        flows = spread + flows[len(levels[depth]) :]
    return flows


def odd(rows):
    return rows | 1


def total(terms):
    result = None
    for term in terms:
        if term is not None:
            result = term if result is None else result + term
    return result


def times(weight, flow):
    return None if flow is None else weight if isinstance(flow, float) else weight * flow


def kernel(devices, wall_devices, planes, vel_hbm, visc_hbm, coef_hbm, out,
           vel, visc, coef, edge, wall_out, got_w, stiff_t, src, src_t, ratio_s, inv_s, head_s, y_s, seg_a, seg_b,
           seg_f, flow, sol_t, sol, rim, rim_t, rim_sol, weigh, coef_s, msg_a, msg_b, msg_c, got_a, got_b, got_c,
           load_sem, wall_send, wall_recv, ring_sem):
    slabs, rows, cells = vel_hbm.shape
    components = slabs // planes
    lines = planes * rows
    groups = lines // LANES
    length = cells // SEGMENTS
    piece = length // PIECES
    pitch = odd(length)
    step = odd(groups)
    me = lax.axis_index("stream")
    wall = lax.axis_index("wall")
    has_below = wall > 0
    has_above = wall < wall_devices - 1
    barrier = pltpu.get_barrier_semaphore()
    edges = [
        pltpu.make_async_copy(vel_hbm.at[:, rows - 8 : rows, :], edge.at[0], load_sem.at[3]),
        pltpu.make_async_copy(vel_hbm.at[:, 0:8, :], edge.at[1], load_sem.at[3]),
    ]
    loads = [
        pltpu.make_async_copy(visc_hbm, visc, load_sem.at[0]),
        pltpu.make_async_copy(coef_hbm, coef, load_sem.at[1]),
    ] + [
        pltpu.make_async_copy(
            vel_hbm.at[:, :, h * LANES : (h + 1) * LANES], vel.at[h, :, 8 : 8 + rows, :], load_sem.at[2])
        for h in range(cells // LANES)
    ]
    for load in edges + loads:
        load.start()

    def await_all(landed, sem):
        pltpu.make_async_copy(landed, landed, sem).wait()

    def around(d):
        return lax.rem(me + d, devices)

    def greet(target):
        for d in range(devices):
            pl.semaphore_signal(
                barrier, inc=1, device_id={"wall": target, "stream": around(d)}, device_id_type=MESH)

    @pl.when(has_below)
    def _():
        greet(wall - 1)

    @pl.when(has_above)
    def _():
        greet(wall + 1)

    for d in range(1, devices):
        pl.semaphore_signal(barrier, inc=1, device_id={"stream": around(d)}, device_id_type=MESH)

    nothing = jnp.zeros((cells // LANES, slabs, 1, LANES), jnp.float32)
    vel[:, :, 7:8, :] = nothing
    vel[:, :, 8 + rows : 9 + rows, :] = nothing
    wall_out[...] = jnp.zeros(wall_out.shape, jnp.float32)
    await_all(edge, load_sem.at[3])
    for a in range(slabs):
        wall_out[0, a : a + 1, :] = edge[0, a, 7:8, :]
        wall_out[1, a : a + 1, :] = edge[1, a, 0:1, :]

    def wall_copy(side, d, target):
        return pltpu.make_async_remote_copy(
            src_ref=wall_out.at[side], dst_ref=got_w.at[side, d],
            send_sem=wall_send.at[side], recv_sem=wall_recv.at[side, min(d, 1)],
            device_id={"wall": target, "stream": around(d)}, device_id_type=MESH)

    def ring_copy(d, source, target, send, recv):
        return pltpu.make_async_remote_copy(
            src_ref=source, dst_ref=target.at[d - 1],
            send_sem=send, recv_sem=recv,
            device_id={"stream": around(d)}, device_id_type=MESH)

    def at_position(i):
        return pl.ds(i, SEGMENTS, stride=pitch)

    def put_segments(buffer, slot, value):
        for g in range(groups):
            buffer[slot, pl.ds(g, SEGMENTS, stride=step), :] = value[g]

    def take_segment(buffer, slot, s):
        return buffer[slot, s * step : s * step + groups, :]

    def spread_rows(target, turned):
        for s in range(SEGMENTS):
            target[s * pitch : s * pitch + length, :] = turned[s * length : (s + 1) * length, :]

    def gather_rows(source):
        return jnp.concatenate([source[s * pitch : s * pitch + length, :] for s in range(SEGMENTS)])

    def factor(source, g):
        one = jnp.ones((SEGMENTS, LANES), jnp.float32)
        excess, reach = [one] * PIECES, [one] * PIECES
        corner = [None] * PIECES
        stiff = [source[at_position(b * piece), :] for b in range(PIECES)]
        starts = list(stiff)
        blocks = []
        for t in range(piece):
            for b in range(PIECES):
                i = b * piece + t
                if t < piece - 1:
                    following = source[at_position(i + 1), :]
                    link = 0.5 * (stiff[b] + following)
                    stiff[b] = following
                    inv = 1.0 / (excess[b] + link)
                    ratio = link * inv
                    ratio_s[i, g] = ratio
                else:
                    inv = 1.0 / excess[b]
                head = reach[b] * inv
                inv_s[i, g] = inv
                head_s[i, g] = head
                corner[b] = head * reach[b] if t == 0 else corner[b] + head * reach[b]
                if t < piece - 1:
                    excess[b] = 1.0 + ratio * excess[b]
                    reach[b] = reach[b] * ratio
                else:
                    blocks.append(((corner[b], head, inv), starts[b], stiff[b]))
        return blocks

    def forward(load, keep, g, fields):
        y = [[None] * fields for _ in range(PIECES)]
        first = [[None] * fields for _ in range(PIECES)]
        final = [[None] * fields for _ in range(PIECES)]
        for t in range(piece):
            for b in range(PIECES):
                i = b * piece + t
                head = head_s[i, g]
                ratio = ratio_s[i - 1, g] if t else None
                for c in range(fields):
                    f = load(c, i)
                    y[b][c] = f + ratio * y[b][c] if t else f
                    keep(c, i, y[b][c])
                    first[b][c] = first[b][c] + head * y[b][c] if t else head * y[b][c]
                    if t == piece - 1:
                        final[b][c] = inv_s[i, g] * y[b][c]
        return first, final

    def backward(spread, kept, put, g):
        for b in range(PIECES):
            now = [None] * len(spread)
            for t in reversed(range(piece)):
                i = b * piece + t
                head = head_s[i, g]
                inv = inv_s[i, g]
                if t < piece - 1:
                    ratio = ratio_s[i, g]
                for f in range(len(spread)):
                    fin, fout = spread[f][b]
                    terms = [times(head, fin)]
                    if kept is not None:
                        terms.append(kept(f, i) * inv)
                    if t < piece - 1:
                        terms.append(ratio * now[f])
                    value = total(terms)
                    if t == piece - 1 and fout is not None:
                        value = value - fout * inv
                    now[f] = value
                    put(f, i, value)

    loads[0].wait()
    parts = []
    for g in range(groups):
        spread_rows(stiff_t.at[g], visc[g * LANES : (g + 1) * LANES, :].T)
        parts.append(factor(stiff_t.at[g], g))
    blocks = [
        (tuple(jnp.stack([p[b][0][q] for p in parts]) for q in range(3)),
         jnp.stack([p[b][1] for p in parts]), jnp.stack([p[b][2] for p in parts]))
        for b in range(PIECES)
    ]
    whole, piece_levels = join_tree(blocks)
    for slot, value in enumerate(whole[0] + whole[1:]):
        put_segments(seg_a, slot, value)
    blocks = []
    for s in range(SEGMENTS):
        v = [take_segment(seg_a, slot, s) for slot in range(5)]
        blocks.append((tuple(v[:3]), v[3], v[4]))
    mine, levels = join_tree(blocks)
    for q, value in enumerate(mine[0] + (mine[1], mine[2])):
        msg_a[q * groups : (q + 1) * groups, :] = value
    zero = jnp.zeros((groups, LANES), jnp.float32)
    unit = jnp.ones((groups, LANES), jnp.float32)

    def solve_fields(chosen):
        for f in chosen:
            if f < components:
                picked = [[j[f] for j in level] for level in jumps]
                flows = down_tree(levels, picked, None, None)
            elif f == components:
                flows = down_tree(levels, None, 1.0, None)
            else:
                flows = down_tree(levels, None, None, 1.0)
            for s, (fin, fout) in enumerate(flows):
                for side, term in enumerate((fin, fout)):
                    term = zero if term is None else unit if isinstance(term, float) else term
                    seg_f[2 * f + side, s * step : s * step + groups, :] = term
        for g in range(groups):
            near = [[tuple(w[g] for w in weights) for weights in level] for level in piece_levels]
            spread = []
            for f in chosen:
                fin, fout = (seg_f[2 * f + side, pl.ds(g, SEGMENTS, stride=step), :] for side in range(2))
                picked = [[j[f][g] for j in level] for level in piece_jumps] if f < components else None
                spread.append(down_tree(near, picked, fin, fout))

            def put(n, i, value, g=g):
                sol_t[chosen[n], g, at_position(i), :] = value

            kept = None if chosen[0] >= components else lambda n, i, g=g: y_s[chosen[n], i, g]
            backward(spread, kept, put, g)
            for f in chosen:
                sol[f, g * LANES : (g + 1) * LANES, :] = gather_rows(sol_t.at[f, g]).T

    solve_fields([components, components + 1])
    ends = [(side, p, p * rows + side * (rows - 1)) for side in range(2) for p in range(planes)]
    for side, p, r in ends:
        for f in range(2):
            e = (f * 2 + side) * planes + p
            msg_c[e : e + 1, :] = sol[components + f, r : r + 1, :]
    beside = jnp.where(has_below, devices, 0) + jnp.where(has_above, devices, 0)
    pl.semaphore_wait(barrier, devices - 1 + beside)

    @pl.when(has_above)
    def _():
        for d in range(devices):
            wall_copy(0, d, wall + 1).start()

    @pl.when(has_below)
    def _():
        for d in range(devices):
            wall_copy(1, d, wall - 1).start()

    @pl.when(jnp.logical_not(has_below))
    def _():
        got_w[0] = jnp.zeros(got_w.shape[1:], jnp.float32)

    @pl.when(jnp.logical_not(has_above))
    def _():
        got_w[1] = jnp.zeros(got_w.shape[1:], jnp.float32)

    for d in range(1, devices):
        ring_copy(d, msg_a, got_a, ring_sem.at[0, 0], ring_sem.at[0, 1]).start()
    for d in range(1, devices):
        ring_copy(d, msg_c, got_c, ring_sem.at[2, 0], ring_sem.at[2, 1]).start()
    loads[1].wait()
    coef_s[...] = jnp.zeros(coef_s.shape, jnp.float32)
    coef_s[0:2, 0:rows] = coef[...]
    slopes = coef_s[...].T
    await_all(vel.at[:, :, 8 : 8 + rows, :], load_sem.at[2])
    for r in range(0, rows, 8):
        up = jnp.broadcast_to(slopes[r : r + 8, 0:1], (8, LANES))
        down = jnp.broadcast_to(slopes[r : r + 8, 1:2], (8, LANES))
        keep = 1.0 - up - down
        for a in range(slabs):
            c, p = a // planes, a % planes
            for h in range(cells // LANES):
                src[c, p * rows + r : p * rows + r + 8, h * LANES : (h + 1) * LANES] = (
                    keep * vel[h, a, 8 + r : 16 + r, :]
                    + up * vel[h, a, 9 + r : 17 + r, :]
                    + down * vel[h, a, 7 + r : 15 + r, :]
                )
    firsts, finals = [], []
    for g in range(groups):
        for c in range(components):
            spread_rows(src_t.at[c, g], src[c, g * LANES : (g + 1) * LANES, :].T)

        def keep_y(c, i, value, g=g):
            y_s[c, i, g] = value

        first, final = forward(lambda c, i, g=g: src_t[c, g, at_position(i), :], keep_y, g, components)
        firsts.append(first)
        finals.append(final)
    values = [
        ([jnp.stack([v[b][c] for v in firsts]) for c in range(components)],
         [jnp.stack([v[b][c] for v in finals]) for c in range(components)])
        for b in range(PIECES)
    ]
    whole, piece_jumps = value_tree(values, piece_levels)
    for slot, value in enumerate(whole[0] + whole[1]):
        put_segments(seg_b, slot, value)
    values = []
    for s in range(SEGMENTS):
        v = [take_segment(seg_b, slot, s) for slot in range(2 * components)]
        values.append((v[:components], v[components:]))
    own, jumps = value_tree(values, levels)
    for q, value in enumerate(own[0] + own[1]):
        msg_b[q * groups : (q + 1) * groups, :] = value
    for d in range(1, devices):
        ring_copy(d, msg_b, got_b, ring_sem.at[1, 0], ring_sem.at[1, 1]).start()
    solve_fields(list(range(components)))
    rim[...] = jnp.ones(rim.shape, jnp.float32)
    for side, p, r in ends:
        for c in range(components):
            e = side * 8 + c * planes + p
            rim[e : e + 1, :] = visc[r : r + 1, :]
    spread_rows(rim_t.at[0], rim[...].T)
    whole, rim_piece_levels = join_tree(factor(rim_t.at[0], groups))
    rim_blocks = whole[0] + whole[1:]
    for slot, value in enumerate(rim_blocks):
        seg_a[slot, 0:SEGMENTS, :] = value
    blocks = []
    for s in range(SEGMENTS):
        v = [seg_a[slot, s : s + 1, :] for slot in range(5)]
        blocks.append((tuple(v[:3]), v[3], v[4]))
    _, rim_levels = join_tree(blocks)

    @pl.when(has_below)
    def _():
        wall_copy(0, 0, wall).wait_recv()

    @pl.when(has_above)
    def _():
        wall_copy(1, 0, wall).wait_recv()

    scales = (slopes[0:1, 1:2], slopes[rows - 1 : rows, 0:1])
    for side in range(2):
        rim[side * 8 : side * 8 + 8, :] = got_w[side, 0] * scales[side]
    spread_rows(rim_t.at[0], rim[...].T)
    held = {}

    def keep_rim(c, i, value):
        held[i] = value

    first, final = forward(lambda c, i: rim_t[0, at_position(i), :], keep_rim, groups, 1)
    whole, rim_piece_jumps = value_tree([(first[b], final[b]) for b in range(PIECES)], rim_piece_levels)
    seg_b[0, 0:SEGMENTS, :] = whole[0][0]
    seg_b[1, 0:SEGMENTS, :] = whole[1][0]
    _, rim_jumps = value_tree(
        [([seg_b[0, s : s + 1, :]], [seg_b[1, s : s + 1, :]]) for s in range(SEGMENTS)], rim_levels)
    picked = [[j[0] for j in level] for level in rim_jumps]
    for s, terms in enumerate(down_tree(rim_levels, picked, None, None)):
        for side, term in enumerate(terms):
            term = jnp.zeros((1, LANES), jnp.float32) if term is None else term
            seg_f[side, s : s + 1, :] = term
    picked = [[j[0] for j in level] for level in rim_piece_jumps]
    spread = [down_tree(rim_piece_levels, picked, seg_f[0, 0:SEGMENTS, :], seg_f[1, 0:SEGMENTS, :])]

    def put_rim(n, i, value):
        rim_t[1, at_position(i), :] = value

    backward(spread, lambda n, i: held[i], put_rim, groups)
    rim_sol[...] = gather_rows(rim_t.at[1]).T
    await_all(got_a, ring_sem.at[0, 1])
    others = []
    for t in range(1, devices):
        slot = devices - t - 1
        v = [got_a[slot, q * groups : (q + 1) * groups, :] for q in range(5)]
        others.append((tuple(v[:3]), v[3], v[4]))
    rest, ring_levels = join_tree(others)
    (m00, m0l, mll), m_first, m_last = mine
    (b00, b0l, bll), b_first, b_last = rest
    out_diag = 2.0 / (m_last + b_first) + mll + b00
    in_diag = 2.0 / (b_last + m_first) + bll + m00
    cross = m0l + b0l
    det = 1.0 / (out_diag * in_diag - cross * cross)
    near_in, near_out, across = out_diag * det, in_diag * det, cross * det

    def put_weights(d, weights):
        for n, value in enumerate(weights):
            for g in range(groups):
                k = 4 * d + n
                weigh[g, k : k + 1, :] = value[g : g + 1]

    put_weights(0, (0.0 - near_in, 0.0 - across, 0.0 - across, 0.0 - near_out))
    to_first = down_tree(ring_levels, None, 1.0, None)
    to_last = down_tree(ring_levels, None, None, 1.0)
    for t in range(1, devices):
        pairs = list(zip(to_first[t - 1], to_last[t - 1]))
        weights = []
        for by_first, by_last in ((across, near_in), (near_out, across)):
            for from_first, from_last in pairs:
                weights.append(0.0 - total((times(by_first, from_first), times(by_last, from_last))))
        put_weights(devices - t, weights)
    row_plane = lax.broadcasted_iota(jnp.int32, (8, 1), 0) % planes

    def by_plane(pick):
        tile = pick(0)
        for p in range(1, planes):
            tile = jnp.where(row_plane == p, pick(p), tile)
        return tile

    turned = [weigh[g].T for g in range(groups)]
    tables = []
    for side in range(2):
        def pick(p):
            r = p * rows + side * (rows - 1)
            line = r % LANES
            return turned[r // LANES][line : line + 1, :]
        tables.append(by_plane(pick) * scales[side])
    await_all(got_b, ring_sem.at[1, 1])
    theirs = []
    for t in range(1, devices):
        slot = devices - t - 1
        v = [got_b[slot, q * groups : (q + 1) * groups, :] for q in range(2 * components)]
        theirs.append((v[:components], v[components:]))
    tail, _ = value_tree(theirs, ring_levels)
    for c in range(components):
        gap_out = own[1][c] - tail[0][c]
        gap_in = tail[1][c] - own[0][c]
        outflow = near_out * gap_out + across * gap_in
        inflow = near_in * gap_in + across * gap_out
        for g in range(groups):
            flow[g, c : c + 1, :] = inflow[g : g + 1]
            flow[g, components + c : components + c + 1, :] = outflow[g : g + 1]

    for g in range(groups):
        span = slice(g * LANES, (g + 1) * LANES)
        columns = flow[g].T
        from_left = sol[components, span, :]
        from_right = sol[components + 1, span, :]
        for c in range(components):
            out[c, span, :] = (
                sol[c, span, :]
                + columns[:, c : c + 1] * from_left
                + columns[:, components + c : components + c + 1] * from_right
            )
    await_all(got_c, ring_sem.at[2, 1])

    def side_rows(d, f, side):
        source = msg_c if d == 0 else got_c.at[d - 1]
        base = (f * 2 + side) * planes
        return by_plane(lambda p: source[base + p : base + p + 1, :])

    weights = {}
    for side in range(2):
        for d in range(devices):
            left, right = side_rows(d, 0, side), side_rows(d, 1, side)
            for way in range(2):
                k = 4 * d + 2 * way
                weights[side, d, way] = tables[side][:, k : k + 1] * left + tables[side][:, k + 1 : k + 2] * right

    for n, sent in enumerate((got_a, got_b, got_c)):
        await_all(sent, ring_sem.at[n, 0])

    @pl.when(has_above)
    def _():
        await_all(got_w.at[0], wall_send.at[0])

    @pl.when(has_below)
    def _():
        await_all(got_w.at[1], wall_send.at[1])

    @pl.when(has_below)
    def _():
        await_all(got_w.at[0, 1:devices], wall_recv.at[0, 1])

    @pl.when(has_above)
    def _():
        await_all(got_w.at[1, 1:devices], wall_recv.at[1, 1])

    for side in range(2):
        ways = []
        for way in range(2):
            sums = total([got_w[side, d] * weights[side, d, way] for d in range(devices)])
            ways.append(jnp.sum(sums, axis=1, keepdims=True))
        added = (
            rim_sol[side * 8 : side * 8 + 8, :] + ways[0] * side_rows(0, 0, side) + ways[1] * side_rows(0, 1, side)
        )
        for c in range(components):
            for p in range(planes):
                r = p * rows + side * (rows - 1)
                e = c * planes + p
                out[c, r : r + 1, :] = out[c, r : r + 1, :] + added[e : e + 1, :]


def shards(devices, wall_devices, velocity, viscosity, y_coef):
    components, planes, rows, cells = velocity.shape
    lines = planes * rows
    slabs = components * planes
    groups = lines // LANES
    length = cells // SEGMENTS
    fields = components + 2
    f32 = jnp.float32
    rows_a, rows_b, rows_c = up8(5 * groups), up8(2 * components * groups), up8(4 * planes)
    peers = devices - 1
    sweeps = (length, groups + 1, SEGMENTS, LANES)
    turned = (SEGMENTS * odd(length), LANES)
    joints = SEGMENTS * odd(groups)
    vmem = pl.BlockSpec(memory_space=pltpu.VMEM)
    result = pl.pallas_call(
        functools.partial(kernel, devices, wall_devices, planes),
        out_shape=jax.ShapeDtypeStruct((components, lines, cells), f32),
        in_specs=[pl.BlockSpec(memory_space=pltpu.HBM)] * 3,
        out_specs=vmem,
        scratch_shapes=[
            pltpu.VMEM((cells // LANES, slabs, rows + 16, LANES), f32),
            pltpu.VMEM((lines, cells), f32),
            pltpu.VMEM(y_coef.shape, f32),
            pltpu.VMEM((2, slabs, 8, cells), f32),
            pltpu.VMEM((2, 8, cells), f32),
            pltpu.VMEM((2, devices, 8, cells), f32),
            pltpu.VMEM((groups,) + turned, f32),
            pltpu.VMEM((components, lines, cells), f32),
            pltpu.VMEM((components, groups) + turned, f32),
            pltpu.VMEM(sweeps, f32),
            pltpu.VMEM(sweeps, f32),
            pltpu.VMEM(sweeps, f32),
            pltpu.VMEM((components, length, groups, SEGMENTS, LANES), f32),
            pltpu.VMEM((5, joints, LANES), f32),
            pltpu.VMEM((2 * components, joints, LANES), f32),
            pltpu.VMEM((2 * fields, joints, LANES), f32),
            pltpu.VMEM((groups, up8(2 * components), LANES), f32),
            pltpu.VMEM((fields, groups) + turned, f32),
            pltpu.VMEM((fields, lines, cells), f32),
            pltpu.VMEM((LANES, cells), f32),
            pltpu.VMEM((2,) + turned, f32),
            pltpu.VMEM((LANES, cells), f32),
            pltpu.VMEM((groups, 4 * devices, LANES), f32),
            pltpu.VMEM((8, -(-rows // LANES) * LANES), f32),
            pltpu.VMEM((rows_a, LANES), f32),
            pltpu.VMEM((rows_b, LANES), f32),
            pltpu.VMEM((rows_c, cells), f32),
            pltpu.VMEM((peers, rows_a, LANES), f32),
            pltpu.VMEM((peers, rows_b, LANES), f32),
            pltpu.VMEM((peers, rows_c, cells), f32),
            pltpu.SemaphoreType.DMA((4,)),
            pltpu.SemaphoreType.DMA((2,)),
            pltpu.SemaphoreType.DMA((2, 2)),
            pltpu.SemaphoreType.DMA((3, 2)),
        ],
        compiler_params=pltpu.CompilerParams(
            collective_id=0, has_side_effects=True, vmem_limit_bytes=40 * 1024 * 1024
        ),
        name="implicit_lines",
    )(
        pltpu.with_memory_space_constraint(velocity.reshape(slabs, rows, cells), pltpu.HBM),
        pltpu.with_memory_space_constraint(viscosity.reshape(lines, cells), pltpu.HBM),
        pltpu.with_memory_space_constraint(y_coef, pltpu.HBM),
    )
    return result.reshape(velocity.shape)


def solution(mesh):
    placed = (P(None, None, "wall", "stream"), P(None, "wall", "stream"), P(None, "wall"))
    return jax.shard_map(
        functools.partial(shards, mesh.shape["stream"], mesh.shape["wall"]),
        mesh=mesh,
        in_specs=placed,
        out_specs=P(None, None, "wall", "stream"),
        check_vma=False,
    )
```

```python
import functools

import jax
import jax.numpy as jnp
from jax import lax
from jax.experimental import pallas as pl
from jax.experimental.pallas import tpu as pltpu
from jax.sharding import PartitionSpec as P

SEGMENTS = 8
PIECES = 4
LANES = 128
MESH = pl.DeviceIdType.MESH


def up8(rows):
    return -(-rows // 8) * 8


def join_matrix(a, b, link):
    a00, a0l, all_ = a
    b00, b0l, bll = b
    gain = link / (1.0 + link * (all_ + b00))
    left = gain * a0l
    right = gain * b0l
    return (a00 - left * a0l, left * b0l, bll - right * b0l), (gain, left, right)


def join_values(a, b, weights):
    _, left, right = weights
    jump = [al - b0 for al, b0 in zip(a[1], b[0])]
    first = [a0 - left * j for a0, j in zip(a[0], jump)]
    last = [bl + right * j for bl, j in zip(b[1], jump)]
    return (first, last), jump


def join_tree(blocks):
    levels = []
    while len(blocks) > 1:
        merged, weights = [], []
        for i in range(0, len(blocks) - 1, 2):
            (ma, fa, la), (mb, fb, lb) = blocks[i], blocks[i + 1]
            m, w = join_matrix(ma, mb, 0.5 * (la + fb))
            merged.append((m, fa, lb))
            weights.append(w)
        if len(blocks) % 2:
            merged.append(blocks[-1])
        levels.append(weights)
        blocks = merged
    return blocks[0], levels


def value_tree(values, levels):
    jumps = []
    for weights in levels:
        merged, jump = [], []
        for i, w in enumerate(weights):
            v, j = join_values(values[2 * i], values[2 * i + 1], w)
            merged.append(v)
            jump.append(j)
        if len(values) % 2:
            merged.append(values[-1])
        jumps.append(jump)
        values = merged
    return values[0], jumps


def down_tree(levels, jumps, inflow, outflow):
    flows = [(inflow, outflow)]
    for depth in reversed(range(len(levels))):
        spread = []
        for i, (gain, left, right) in enumerate(levels[depth]):
            fin, fout = flows[i]
            middle = None
            for term, weight in ((fin, left), (fout, right)):
                if term is not None:
                    part = weight if isinstance(term, float) else term * weight
                    middle = part if middle is None else middle + part
            if jumps is not None:
                part = gain * jumps[depth][i]
                middle = part if middle is None else middle + part
            spread += [(fin, middle), (middle, fout)]
        flows = spread + flows[len(levels[depth]) :]
    return flows


def odd(rows):
    return rows | 1


def total(terms):
    result = None
    for term in terms:
        if term is not None:
            result = term if result is None else result + term
    return result


def times(weight, flow):
    return None if flow is None else weight if isinstance(flow, float) else weight * flow


def kernel(devices, wall_devices, planes, vel_hbm, visc_hbm, coef_hbm, out,
           vel, visc, coef, edge, wall_out, got_w, got_s, stiff_t, src, src_t, ratio_s, inv_s, head_s, y_s, seg_a, seg_b,
           seg_f, flow, sol_t, sol, rim, rim_t, rim_sol, weigh, coef_s, msg_a, msg_b, msg_c, msg_d, got_a, got_b, got_c, got_d,
           load_sem, wall_send, wall_recv, ring_sem):
    slabs, rows, cells = vel_hbm.shape
    components = slabs // planes
    lines = planes * rows
    groups = lines // LANES
    length = cells // SEGMENTS
    piece = length // PIECES
    pitch = odd(length)
    step = odd(groups)
    me = lax.axis_index("stream")
    wall = lax.axis_index("wall")
    has_below = wall > 0
    has_above = wall < wall_devices - 1
    second = lax.rem(me, 2)
    is_first, is_second = second == 0, second == 1
    barrier = pltpu.get_barrier_semaphore()
    edges = [
        pltpu.make_async_copy(vel_hbm.at[:, rows - 8 : rows, :], edge.at[0], load_sem.at[3]),
        pltpu.make_async_copy(vel_hbm.at[:, 0:8, :], edge.at[1], load_sem.at[3]),
    ]
    loads = [
        pltpu.make_async_copy(visc_hbm, visc, load_sem.at[0]),
        pltpu.make_async_copy(coef_hbm, coef, load_sem.at[1]),
    ] + [
        pltpu.make_async_copy(
            vel_hbm.at[:, :, h * LANES : (h + 1) * LANES], vel.at[h, :, 8 : 8 + rows, :], load_sem.at[2])
        for h in range(cells // LANES)
    ]
    for load in edges + loads:
        load.start()

    def await_all(landed, sem):
        pltpu.make_async_copy(landed, landed, sem).wait()

    def around(d):
        return lax.rem(me + d, devices)

    def greet(target):
        pl.semaphore_signal(barrier, inc=1, device_id={"wall": target}, device_id_type=MESH)

        @pl.when(is_second)
        def _():
            pl.semaphore_signal(
                barrier, inc=1, device_id={"wall": target, "stream": me - 1}, device_id_type=MESH)

    got_d[...] = jnp.zeros(got_d.shape, jnp.float32)
    msg_d[...] = jnp.zeros(msg_d.shape, jnp.float32)

    @pl.when(has_below)
    def _():
        greet(wall - 1)

    @pl.when(has_above)
    def _():
        greet(wall + 1)

    for d in range(1, devices):
        pl.semaphore_signal(barrier, inc=1, device_id={"stream": around(d)}, device_id_type=MESH)

    nothing = jnp.zeros((cells // LANES, slabs, 1, LANES), jnp.float32)
    vel[:, :, 7:8, :] = nothing
    vel[:, :, 8 + rows : 9 + rows, :] = nothing
    wall_out[...] = jnp.zeros(wall_out.shape, jnp.float32)
    await_all(edge, load_sem.at[3])
    for a in range(slabs):
        wall_out[0, a : a + 1, :] = edge[0, a, 7:8, :]
        wall_out[1, a : a + 1, :] = edge[1, a, 0:1, :]

    def wall_copy(side, target):
        return pltpu.make_async_remote_copy(
            src_ref=wall_out.at[side], dst_ref=got_w.at[side],
            send_sem=wall_send.at[side], recv_sem=wall_recv.at[side],
            device_id={"wall": target}, device_id_type=MESH)

    def beside_copy(side, target):
        return pltpu.make_async_remote_copy(
            src_ref=wall_out.at[side], dst_ref=got_s.at[side],
            send_sem=wall_send.at[side], recv_sem=wall_recv.at[side],
            device_id={"wall": target, "stream": me + 1 - 2 * second}, device_id_type=MESH)

    rows_copy = pltpu.make_async_remote_copy(
        src_ref=msg_c, dst_ref=got_c, send_sem=ring_sem.at[2, 0], recv_sem=ring_sem.at[2, 1],
        device_id={"stream": me + 1 - 2 * second}, device_id_type=MESH)

    def ring_copy(d, source, target, send, recv):
        return pltpu.make_async_remote_copy(
            src_ref=source, dst_ref=target.at[d - 1],
            send_sem=send, recv_sem=recv,
            device_id={"stream": around(d)}, device_id_type=MESH)

    def at_position(i):
        return pl.ds(i, SEGMENTS, stride=pitch)

    def put_segments(buffer, slot, value):
        for g in range(groups):
            buffer[slot, pl.ds(g, SEGMENTS, stride=step), :] = value[g]

    def take_segment(buffer, slot, s):
        return buffer[slot, s * step : s * step + groups, :]

    def spread_rows(target, turned):
        for s in range(SEGMENTS):
            target[s * pitch : s * pitch + length, :] = turned[s * length : (s + 1) * length, :]

    def gather_rows(source):
        return jnp.concatenate([source[s * pitch : s * pitch + length, :] for s in range(SEGMENTS)])

    def factor(source, g):
        one = jnp.ones((SEGMENTS, LANES), jnp.float32)
        excess, reach = [one] * PIECES, [one] * PIECES
        corner = [None] * PIECES
        stiff = [source[at_position(b * piece), :] for b in range(PIECES)]
        starts = list(stiff)
        blocks = []
        for t in range(piece):
            for b in range(PIECES):
                i = b * piece + t
                if t < piece - 1:
                    following = source[at_position(i + 1), :]
                    link = 0.5 * (stiff[b] + following)
                    stiff[b] = following
                    inv = 1.0 / (excess[b] + link)
                    ratio = link * inv
                    ratio_s[i, g] = ratio
                else:
                    inv = 1.0 / excess[b]
                head = reach[b] * inv
                inv_s[i, g] = inv
                head_s[i, g] = head
                corner[b] = head * reach[b] if t == 0 else corner[b] + head * reach[b]
                if t < piece - 1:
                    excess[b] = 1.0 + ratio * excess[b]
                    reach[b] = reach[b] * ratio
                else:
                    blocks.append(((corner[b], head, inv), starts[b], stiff[b]))
        return blocks

    def forward(load, keep, g, fields):
        y = [[None] * fields for _ in range(PIECES)]
        first = [[None] * fields for _ in range(PIECES)]
        final = [[None] * fields for _ in range(PIECES)]
        for t in range(piece):
            for b in range(PIECES):
                i = b * piece + t
                head = head_s[i, g]
                ratio = ratio_s[i - 1, g] if t else None
                for c in range(fields):
                    f = load(c, i)
                    y[b][c] = f + ratio * y[b][c] if t else f
                    keep(c, i, y[b][c])
                    first[b][c] = first[b][c] + head * y[b][c] if t else head * y[b][c]
                    if t == piece - 1:
                        final[b][c] = inv_s[i, g] * y[b][c]
        return first, final

    def backward(spread, kept, put, g):
        for b in range(PIECES):
            now = [None] * len(spread)
            for t in reversed(range(piece)):
                i = b * piece + t
                head = head_s[i, g]
                inv = inv_s[i, g]
                if t < piece - 1:
                    ratio = ratio_s[i, g]
                for f in range(len(spread)):
                    fin, fout = spread[f][b]
                    terms = [times(head, fin)]
                    if kept is not None:
                        terms.append(kept(f, i) * inv)
                    if t < piece - 1:
                        terms.append(ratio * now[f])
                    value = total(terms)
                    if t == piece - 1 and fout is not None:
                        value = value - fout * inv
                    now[f] = value
                    put(f, i, value)

    loads[0].wait()
    parts = []
    for g in range(groups):
        spread_rows(stiff_t.at[g], visc[g * LANES : (g + 1) * LANES, :].T)
        parts.append(factor(stiff_t.at[g], g))
    blocks = [
        (tuple(jnp.stack([p[b][0][q] for p in parts]) for q in range(3)),
         jnp.stack([p[b][1] for p in parts]), jnp.stack([p[b][2] for p in parts]))
        for b in range(PIECES)
    ]
    whole, piece_levels = join_tree(blocks)
    for slot, value in enumerate(whole[0] + whole[1:]):
        put_segments(seg_a, slot, value)
    blocks = []
    for s in range(SEGMENTS):
        v = [take_segment(seg_a, slot, s) for slot in range(5)]
        blocks.append((tuple(v[:3]), v[3], v[4]))
    mine, levels = join_tree(blocks)
    for q, value in enumerate(mine[0] + (mine[1], mine[2])):
        msg_a[q * groups : (q + 1) * groups, :] = value

    each = 2 - second
    beside = jnp.where(has_below, each, 0) + jnp.where(has_above, each, 0)
    pl.semaphore_wait(barrier, devices - 1 + beside)

    def send_rows(side, target):
        wall_copy(side, target).start()

        @pl.when(is_first)
        def _():
            beside_copy(side, target).start()

    @pl.when(has_above)
    def _():
        send_rows(0, wall + 1)

    @pl.when(has_below)
    def _():
        send_rows(1, wall - 1)

    @pl.when(jnp.logical_not(has_below))
    def _():
        got_w[0] = jnp.zeros(got_w.shape[1:], jnp.float32)
        got_s[0] = jnp.zeros(got_w.shape[1:], jnp.float32)

    @pl.when(jnp.logical_not(has_above))
    def _():
        got_w[1] = jnp.zeros(got_w.shape[1:], jnp.float32)
        got_s[1] = jnp.zeros(got_w.shape[1:], jnp.float32)

    for d in range(1, devices):
        ring_copy(d, msg_a, got_a, ring_sem.at[0, 0], ring_sem.at[0, 1]).start()
    zero = jnp.zeros((groups, LANES), jnp.float32)
    unit = jnp.ones((groups, LANES), jnp.float32)

    def solve_fields(chosen):
        for f in chosen:
            if f < components:
                picked = [[j[f] for j in level] for level in jumps]
                flows = down_tree(levels, picked, None, None)
            elif f == components:
                flows = down_tree(levels, None, 1.0, None)
            else:
                flows = down_tree(levels, None, None, 1.0)
            for s, (fin, fout) in enumerate(flows):
                for side, term in enumerate((fin, fout)):
                    term = zero if term is None else unit if isinstance(term, float) else term
                    seg_f[2 * f + side, s * step : s * step + groups, :] = term
        for g in range(groups):
            near = [[tuple(w[g] for w in weights) for weights in level] for level in piece_levels]
            spread = []
            for f in chosen:
                fin, fout = (seg_f[2 * f + side, pl.ds(g, SEGMENTS, stride=step), :] for side in range(2))
                picked = [[j[f][g] for j in level] for level in piece_jumps] if f < components else None
                spread.append(down_tree(near, picked, fin, fout))

            def put(n, i, value, g=g):
                sol_t[chosen[n], g, at_position(i), :] = value

            kept = None if chosen[0] >= components else lambda n, i, g=g: y_s[chosen[n], i, g]
            backward(spread, kept, put, g)
            for f in chosen:
                sol[f, g * LANES : (g + 1) * LANES, :] = gather_rows(sol_t.at[f, g]).T

    solve_fields([components, components + 1])
    ends = [(side, p, p * rows + side * (rows - 1)) for side in range(2) for p in range(planes)]
    for side, p, r in ends:
        for f in range(2):
            e = (f * 2 + side) * planes + p
            msg_c[e : e + 1, :] = sol[components + f, r : r + 1, :]
    @pl.when(is_first)
    def _():
        rows_copy.start()

    row_plane = lax.broadcasted_iota(jnp.int32, (8, 1), 0) % planes

    def by_plane(pick):
        tile = pick(0)
        for p in range(1, planes):
            tile = jnp.where(row_plane == p, pick(p), tile)
        return tile

    def side_rows(source, f, side):
        base = (f * 2 + side) * planes
        return by_plane(lambda p: source[base + p : base + p + 1, :])
    loads[1].wait()
    coef_s[...] = jnp.zeros(coef_s.shape, jnp.float32)
    coef_s[0:2, 0:rows] = coef[...]
    slopes = coef_s[...].T
    await_all(vel.at[:, :, 8 : 8 + rows, :], load_sem.at[2])
    for r in range(0, rows, 8):
        up = jnp.broadcast_to(slopes[r : r + 8, 0:1], (8, LANES))
        down = jnp.broadcast_to(slopes[r : r + 8, 1:2], (8, LANES))
        keep = 1.0 - up - down
        for a in range(slabs):
            c, p = a // planes, a % planes
            for h in range(cells // LANES):
                src[c, p * rows + r : p * rows + r + 8, h * LANES : (h + 1) * LANES] = (
                    keep * vel[h, a, 8 + r : 16 + r, :]
                    + up * vel[h, a, 9 + r : 17 + r, :]
                    + down * vel[h, a, 7 + r : 15 + r, :]
                )
    firsts, finals = [], []
    for g in range(groups):
        for c in range(components):
            spread_rows(src_t.at[c, g], src[c, g * LANES : (g + 1) * LANES, :].T)

        def keep_y(c, i, value, g=g):
            y_s[c, i, g] = value

        first, final = forward(lambda c, i, g=g: src_t[c, g, at_position(i), :], keep_y, g, components)
        firsts.append(first)
        finals.append(final)
    values = [
        ([jnp.stack([v[b][c] for v in firsts]) for c in range(components)],
         [jnp.stack([v[b][c] for v in finals]) for c in range(components)])
        for b in range(PIECES)
    ]
    whole, piece_jumps = value_tree(values, piece_levels)
    for slot, value in enumerate(whole[0] + whole[1]):
        put_segments(seg_b, slot, value)
    values = []
    for s in range(SEGMENTS):
        v = [take_segment(seg_b, slot, s) for slot in range(2 * components)]
        values.append((v[:components], v[components:]))
    own, jumps = value_tree(values, levels)
    for q, value in enumerate(own[0] + own[1]):
        msg_b[q * groups : (q + 1) * groups, :] = value
    for d in range(1, devices):
        ring_copy(d, msg_b, got_b, ring_sem.at[1, 0], ring_sem.at[1, 1]).start()
    @pl.when(is_second)
    def _():
        rows_copy.wait_recv()

        @pl.when(has_below)
        def _():
            await_all(got_w, wall_recv.at[0])

        @pl.when(has_above)
        def _():
            await_all(got_w, wall_recv.at[1])

        lane_kind = lax.broadcasted_iota(jnp.int32, (8, LANES), 1) % 4
        for side in range(2):
            tile = None
            for n, (halo, source) in enumerate(((got_w, msg_c), (got_s, got_c))):
                for f in range(2):
                    value = jnp.sum(halo[side] * side_rows(source, f, side), axis=1, keepdims=True)
                    value = jnp.broadcast_to(value, (8, LANES))
                    tile = value if tile is None else jnp.where(lane_kind == 2 * n + f, value, tile)
            msg_d[side * 8 : side * 8 + 8, :] = tile
        for d in range(1, devices):
            ring_copy(d, msg_d, got_d, ring_sem.at[3, 0], ring_sem.at[3, 1]).start()
    solve_fields(list(range(components)))
    rim[...] = jnp.ones(rim.shape, jnp.float32)
    for side, p, r in ends:
        for c in range(components):
            e = side * 8 + c * planes + p
            rim[e : e + 1, :] = visc[r : r + 1, :]
    spread_rows(rim_t.at[0], rim[...].T)
    whole, rim_piece_levels = join_tree(factor(rim_t.at[0], groups))
    rim_blocks = whole[0] + whole[1:]
    for slot, value in enumerate(rim_blocks):
        seg_a[slot, 0:SEGMENTS, :] = value
    blocks = []
    for s in range(SEGMENTS):
        v = [seg_a[slot, s : s + 1, :] for slot in range(5)]
        blocks.append((tuple(v[:3]), v[3], v[4]))
    _, rim_levels = join_tree(blocks)

    scales = (slopes[0:1, 1:2], slopes[rows - 1 : rows, 0:1])
    await_all(got_a, ring_sem.at[0, 1])
    others = []
    for t in range(1, devices):
        slot = devices - t - 1
        v = [got_a[slot, q * groups : (q + 1) * groups, :] for q in range(5)]
        others.append((tuple(v[:3]), v[3], v[4]))
    rest, ring_levels = join_tree(others)
    (m00, m0l, mll), m_first, m_last = mine
    (b00, b0l, bll), b_first, b_last = rest
    out_diag = 2.0 / (m_last + b_first) + mll + b00
    in_diag = 2.0 / (b_last + m_first) + bll + m00
    cross = m0l + b0l
    det = 1.0 / (out_diag * in_diag - cross * cross)
    near_in, near_out, across = out_diag * det, in_diag * det, cross * det

    def put_weights(leaf, weights):
        for way in range(2):
            for f in range(2):
                for n in range(2):
                    k = 4 * ((leaf - n) % devices) + 2 * n + f
                    for g in range(groups):
                        weigh[way, g, k : k + 1, :] = weights[way][f][g : g + 1]

    put_weights(0, ((0.0 - near_in, 0.0 - across), (0.0 - across, 0.0 - near_out)))
    to_first = down_tree(ring_levels, None, 1.0, None)
    to_last = down_tree(ring_levels, None, None, 1.0)
    for t in range(1, devices):
        pairs = list(zip(to_first[t - 1], to_last[t - 1]))
        put_weights(devices - t, [
            [0.0 - total((times(by_first, from_first), times(by_last, from_last))) for from_first, from_last in pairs]
            for by_first, by_last in ((across, near_in), (near_out, across))
        ])
    tables = {}
    for way in range(2):
        turned = [weigh[way, g].T for g in range(groups)]
        for side in range(2):
            def pick(p):
                r = p * rows + side * (rows - 1)
                line = r % LANES
                return turned[r // LANES][line : line + 1, :]
            tables[side, way] = by_plane(pick) * scales[side]
    await_all(got_b, ring_sem.at[1, 1])
    theirs = []
    for t in range(1, devices):
        slot = devices - t - 1
        v = [got_b[slot, q * groups : (q + 1) * groups, :] for q in range(2 * components)]
        theirs.append((v[:components], v[components:]))
    tail, _ = value_tree(theirs, ring_levels)
    for c in range(components):
        gap_out = own[1][c] - tail[0][c]
        gap_in = tail[1][c] - own[0][c]
        outflow = near_out * gap_out + across * gap_in
        inflow = near_in * gap_in + across * gap_out
        for g in range(groups):
            flow[g, c : c + 1, :] = inflow[g : g + 1]
            flow[g, components + c : components + c + 1, :] = outflow[g : g + 1]

    for g in range(groups):
        span = slice(g * LANES, (g + 1) * LANES)
        columns = flow[g].T
        from_left = sol[components, span, :]
        from_right = sol[components + 1, span, :]
        for c in range(components):
            out[c, span, :] = (
                sol[c, span, :]
                + columns[:, c : c + 1] * from_left
                + columns[:, components + c : components + c + 1] * from_right
            )

    @pl.when(jnp.logical_and(is_first, has_below))
    def _():
        wall_copy(0, wall).wait_recv()

    @pl.when(jnp.logical_and(is_first, has_above))
    def _():
        wall_copy(1, wall).wait_recv()

    for side in range(2):
        rim[side * 8 : side * 8 + 8, :] = got_w[side] * scales[side]
    spread_rows(rim_t.at[0], rim[...].T)
    held = {}

    def keep_rim(c, i, value):
        held[i] = value

    first, final = forward(lambda c, i: rim_t[0, at_position(i), :], keep_rim, groups, 1)
    whole, rim_piece_jumps = value_tree([(first[b], final[b]) for b in range(PIECES)], rim_piece_levels)
    seg_b[0, 0:SEGMENTS, :] = whole[0][0]
    seg_b[1, 0:SEGMENTS, :] = whole[1][0]
    _, rim_jumps = value_tree(
        [([seg_b[0, s : s + 1, :]], [seg_b[1, s : s + 1, :]]) for s in range(SEGMENTS)], rim_levels)
    picked = [[j[0] for j in level] for level in rim_jumps]
    for s, terms in enumerate(down_tree(rim_levels, picked, None, None)):
        for side, term in enumerate(terms):
            term = jnp.zeros((1, LANES), jnp.float32) if term is None else term
            seg_f[side, s : s + 1, :] = term
    picked = [[j[0] for j in level] for level in rim_piece_jumps]
    spread = [down_tree(rim_piece_levels, picked, seg_f[0, 0:SEGMENTS, :], seg_f[1, 0:SEGMENTS, :])]

    def put_rim(n, i, value):
        rim_t[1, at_position(i), :] = value

    backward(spread, lambda n, i: held[i], put_rim, groups)
    rim_sol[...] = gather_rows(rim_t.at[1]).T
    for n, sent in enumerate((got_a, got_b)):
        await_all(sent, ring_sem.at[n, 0])

    @pl.when(is_first)
    def _():
        rows_copy.wait_send()

        @pl.when(has_above)
        def _():
            await_all(got_w, wall_send.at[0])

        @pl.when(has_below)
        def _():
            await_all(got_w, wall_send.at[1])

        await_all(got_d.at[0 : devices // 2], ring_sem.at[3, 1])

    @pl.when(is_second)
    def _():
        @pl.when(has_above)
        def _():
            await_all(got_w.at[0], wall_send.at[0])

        @pl.when(has_below)
        def _():
            await_all(got_w.at[1], wall_send.at[1])

        await_all(got_d, ring_sem.at[3, 0])
        await_all(got_d.at[0 : devices // 2 - 1], ring_sem.at[3, 1])

    lane_slot = lax.broadcasted_iota(jnp.int32, (8, 4 * devices), 1) // 4
    for side in range(2):
        held_rows = slice(side * 8, side * 8 + 8)
        mix = jnp.where(is_second, msg_d[held_rows, 0 : 4 * devices], 0.0)
        for d in range(1, devices):
            mix = jnp.where(lane_slot == d, got_d[d - 1, held_rows, 0 : 4 * devices], mix)
        ways = [jnp.sum(mix * tables[side, way], axis=1, keepdims=True) for way in range(2)]
        added = (
            rim_sol[side * 8 : side * 8 + 8, :] + ways[0] * side_rows(msg_c, 0, side) + ways[1] * side_rows(msg_c, 1, side)
        )
        for c in range(components):
            for p in range(planes):
                r = p * rows + side * (rows - 1)
                e = c * planes + p
                out[c, r : r + 1, :] = out[c, r : r + 1, :] + added[e : e + 1, :]


def shards(devices, wall_devices, velocity, viscosity, y_coef):
    components, planes, rows, cells = velocity.shape
    lines = planes * rows
    slabs = components * planes
    groups = lines // LANES
    length = cells // SEGMENTS
    fields = components + 2
    f32 = jnp.float32
    rows_a, rows_b, rows_c = up8(5 * groups), up8(2 * components * groups), up8(4 * planes)
    peers = devices - 1
    sweeps = (length, groups + 1, SEGMENTS, LANES)
    turned = (SEGMENTS * odd(length), LANES)
    joints = SEGMENTS * odd(groups)
    vmem = pl.BlockSpec(memory_space=pltpu.VMEM)
    result = pl.pallas_call(
        functools.partial(kernel, devices, wall_devices, planes),
        out_shape=jax.ShapeDtypeStruct((components, lines, cells), f32),
        in_specs=[pl.BlockSpec(memory_space=pltpu.HBM)] * 3,
        out_specs=vmem,
        scratch_shapes=[
            pltpu.VMEM((cells // LANES, slabs, rows + 16, LANES), f32),
            pltpu.VMEM((lines, cells), f32),
            pltpu.VMEM(y_coef.shape, f32),
            pltpu.VMEM((2, slabs, 8, cells), f32),
            pltpu.VMEM((2, 8, cells), f32),
            pltpu.VMEM((2, 8, cells), f32),
            pltpu.VMEM((2, 8, cells), f32),
            pltpu.VMEM((groups,) + turned, f32),
            pltpu.VMEM((components, lines, cells), f32),
            pltpu.VMEM((components, groups) + turned, f32),
            pltpu.VMEM(sweeps, f32),
            pltpu.VMEM(sweeps, f32),
            pltpu.VMEM(sweeps, f32),
            pltpu.VMEM((components, length, groups, SEGMENTS, LANES), f32),
            pltpu.VMEM((5, joints, LANES), f32),
            pltpu.VMEM((2 * components, joints, LANES), f32),
            pltpu.VMEM((2 * fields, joints, LANES), f32),
            pltpu.VMEM((groups, up8(2 * components), LANES), f32),
            pltpu.VMEM((fields, groups) + turned, f32),
            pltpu.VMEM((fields, lines, cells), f32),
            pltpu.VMEM((LANES, cells), f32),
            pltpu.VMEM((2,) + turned, f32),
            pltpu.VMEM((LANES, cells), f32),
            pltpu.VMEM((2, groups, 4 * devices, LANES), f32),
            pltpu.VMEM((8, -(-rows // LANES) * LANES), f32),
            pltpu.VMEM((rows_a, LANES), f32),
            pltpu.VMEM((rows_b, LANES), f32),
            pltpu.VMEM((rows_c, cells), f32),
            pltpu.VMEM((16, LANES), f32),
            pltpu.VMEM((peers, rows_a, LANES), f32),
            pltpu.VMEM((peers, rows_b, LANES), f32),
            pltpu.VMEM((rows_c, cells), f32),
            pltpu.VMEM((peers, 16, LANES), f32),
            pltpu.SemaphoreType.DMA((4,)),
            pltpu.SemaphoreType.DMA((2,)),
            pltpu.SemaphoreType.DMA((2,)),
            pltpu.SemaphoreType.DMA((4, 2)),
        ],
        compiler_params=pltpu.CompilerParams(
            collective_id=0, has_side_effects=True, vmem_limit_bytes=40 * 1024 * 1024
        ),
        name="implicit_lines",
    )(
        pltpu.with_memory_space_constraint(velocity.reshape(slabs, rows, cells), pltpu.HBM),
        pltpu.with_memory_space_constraint(viscosity.reshape(lines, cells), pltpu.HBM),
        pltpu.with_memory_space_constraint(y_coef, pltpu.HBM),
    )
    return result.reshape(velocity.shape)


def solution(mesh):
    placed = (P(None, None, "wall", "stream"), P(None, "wall", "stream"), P(None, "wall"))
    return jax.shard_map(
        functools.partial(shards, mesh.shape["stream"], mesh.shape["wall"]),
        mesh=mesh,
        in_specs=placed,
        out_specs=P(None, None, "wall", "stream"),
        check_vma=False,
    )
```

```python
import functools

import jax
import jax.numpy as jnp
from jax import lax
from jax.experimental import pallas as pl
from jax.experimental.pallas import tpu as pltpu
from jax.sharding import PartitionSpec as P

SEGMENTS = 8
PIECES = 4
LANES = 128
MESH = pl.DeviceIdType.MESH


def up8(rows):
    return -(-rows // 8) * 8


def join_matrix(a, b, link):
    a00, a0l, all_ = a
    b00, b0l, bll = b
    gain = link / (1.0 + link * (all_ + b00))
    left = gain * a0l
    right = gain * b0l
    return (a00 - left * a0l, left * b0l, bll - right * b0l), (gain, left, right)


def join_values(a, b, weights):
    _, left, right = weights
    jump = [al - b0 for al, b0 in zip(a[1], b[0])]
    first = [a0 - left * j for a0, j in zip(a[0], jump)]
    last = [bl + right * j for bl, j in zip(b[1], jump)]
    return (first, last), jump


def join_tree(blocks):
    levels = []
    while len(blocks) > 1:
        merged, weights = [], []
        for i in range(0, len(blocks) - 1, 2):
            (ma, fa, la), (mb, fb, lb) = blocks[i], blocks[i + 1]
            m, w = join_matrix(ma, mb, 0.5 * (la + fb))
            merged.append((m, fa, lb))
            weights.append(w)
        if len(blocks) % 2:
            merged.append(blocks[-1])
        levels.append(weights)
        blocks = merged
    return blocks[0], levels


def value_tree(values, levels):
    jumps = []
    for weights in levels:
        merged, jump = [], []
        for i, w in enumerate(weights):
            v, j = join_values(values[2 * i], values[2 * i + 1], w)
            merged.append(v)
            jump.append(j)
        if len(values) % 2:
            merged.append(values[-1])
        jumps.append(jump)
        values = merged
    return values[0], jumps


def down_tree(levels, jumps, inflow, outflow):
    flows = [(inflow, outflow)]
    for depth in reversed(range(len(levels))):
        spread = []
        for i, (gain, left, right) in enumerate(levels[depth]):
            fin, fout = flows[i]
            middle = None
            for term, weight in ((fin, left), (fout, right)):
                if term is not None:
                    part = weight if isinstance(term, float) else term * weight
                    middle = part if middle is None else middle + part
            if jumps is not None:
                part = gain * jumps[depth][i]
                middle = part if middle is None else middle + part
            spread += [(fin, middle), (middle, fout)]
        flows = spread + flows[len(levels[depth]) :]
    return flows


def odd(rows):
    return rows | 1


def total(terms):
    result = None
    for term in terms:
        if term is not None:
            result = term if result is None else result + term
    return result


def times(weight, flow):
    return None if flow is None else weight if isinstance(flow, float) else weight * flow


def kernel(devices, wall_devices, planes, vel_hbm, visc_hbm, coef_hbm, out,
           vel, visc, coef, edge, wall_out, got_w, got_s, stiff_t, src, src_t, ratio_s, inv_s, head_s, y_s, seg_a, seg_b,
           seg_f, flow, sol_t, sol, rim, rim_t, rim_sol, weigh, coef_s, msg_a, msg_b, msg_c, msg_d, got_a, got_b, got_c, got_d,
           load_sem, wall_send, wall_recv, ring_sem):
    slabs, rows, cells = vel_hbm.shape
    components = slabs // planes
    lines = planes * rows
    groups = lines // LANES
    length = cells // SEGMENTS
    piece = length // PIECES
    pitch = odd(length)
    step = odd(groups)
    me = lax.axis_index("stream")
    wall = lax.axis_index("wall")
    has_below = wall > 0
    has_above = wall < wall_devices - 1
    second = lax.rem(me, 2)
    is_first, is_second = second == 0, second == 1
    barrier = pltpu.get_barrier_semaphore()
    edges = [
        pltpu.make_async_copy(vel_hbm.at[:, rows - 8 : rows, :], edge.at[0], load_sem.at[3]),
        pltpu.make_async_copy(vel_hbm.at[:, 0:8, :], edge.at[1], load_sem.at[3]),
    ]
    loads = [
        pltpu.make_async_copy(visc_hbm, visc, load_sem.at[0]),
        pltpu.make_async_copy(coef_hbm, coef, load_sem.at[1]),
    ] + [
        pltpu.make_async_copy(
            vel_hbm.at[:, :, h * LANES : (h + 1) * LANES], vel.at[h, :, 8 : 8 + rows, :], load_sem.at[2])
        for h in range(cells // LANES)
    ]
    def await_all(landed, sem):
        pltpu.make_async_copy(landed, landed, sem).wait()

    def around(d):
        return lax.rem(me + d, devices)

    def greet(target):
        pl.semaphore_signal(barrier, inc=1, device_id={"wall": target}, device_id_type=MESH)

        @pl.when(is_second)
        def _():
            pl.semaphore_signal(
                barrier, inc=1, device_id={"wall": target, "stream": me - 1}, device_id_type=MESH)

    got_d[...] = jnp.zeros(got_d.shape, jnp.float32)
    msg_d[...] = jnp.zeros(msg_d.shape, jnp.float32)

    @pl.when(has_below)
    def _():
        greet(wall - 1)

    @pl.when(has_above)
    def _():
        greet(wall + 1)

    for d in sorted(range(1, devices), key=lambda d: -min(d, devices - d)):
        pl.semaphore_signal(barrier, inc=1, device_id={"stream": around(d)}, device_id_type=MESH)

    for load in edges + loads:
        load.start()

    nothing = jnp.zeros((cells // LANES, slabs, 1, LANES), jnp.float32)
    vel[:, :, 7:8, :] = nothing
    vel[:, :, 8 + rows : 9 + rows, :] = nothing
    wall_out[...] = jnp.zeros(wall_out.shape, jnp.float32)
    await_all(edge, load_sem.at[3])
    for a in range(slabs):
        wall_out[0, a : a + 1, :] = edge[0, a, 7:8, :]
        wall_out[1, a : a + 1, :] = edge[1, a, 0:1, :]

    def wall_copy(side, target):
        return pltpu.make_async_remote_copy(
            src_ref=wall_out.at[side], dst_ref=got_w.at[side],
            send_sem=wall_send.at[side], recv_sem=wall_recv.at[side],
            device_id={"wall": target}, device_id_type=MESH)

    def beside_copy(side, target):
        return pltpu.make_async_remote_copy(
            src_ref=wall_out.at[side], dst_ref=got_s.at[side],
            send_sem=wall_send.at[side], recv_sem=wall_recv.at[side],
            device_id={"wall": target, "stream": me + 1 - 2 * second}, device_id_type=MESH)

    rows_copy = pltpu.make_async_remote_copy(
        src_ref=msg_c, dst_ref=got_c, send_sem=ring_sem.at[2, 0], recv_sem=ring_sem.at[2, 1],
        device_id={"stream": me + 1 - 2 * second}, device_id_type=MESH)

    def ring_copy(d, source, target, send, recv):
        return pltpu.make_async_remote_copy(
            src_ref=source, dst_ref=target.at[d - 1],
            send_sem=send, recv_sem=recv,
            device_id={"stream": around(d)}, device_id_type=MESH)

    def at_position(i):
        return pl.ds(i, SEGMENTS, stride=pitch)

    def put_segments(buffer, slot, value):
        for g in range(groups):
            buffer[slot, pl.ds(g, SEGMENTS, stride=step), :] = value[g]

    def take_segment(buffer, slot, s):
        return buffer[slot, s * step : s * step + groups, :]

    def spread_rows(target, turned):
        for s in range(SEGMENTS):
            target[s * pitch : s * pitch + length, :] = turned[s * length : (s + 1) * length, :]

    def gather_rows(source):
        return jnp.concatenate([source[s * pitch : s * pitch + length, :] for s in range(SEGMENTS)])

    def factor(source, g):
        one = jnp.ones((SEGMENTS, LANES), jnp.float32)
        excess, reach = [one] * PIECES, [one] * PIECES
        corner = [None] * PIECES
        stiff = [source[at_position(b * piece), :] for b in range(PIECES)]
        starts = list(stiff)
        blocks = []
        for t in range(piece):
            for b in range(PIECES):
                i = b * piece + t
                if t < piece - 1:
                    following = source[at_position(i + 1), :]
                    link = 0.5 * (stiff[b] + following)
                    stiff[b] = following
                    inv = 1.0 / (excess[b] + link)
                    ratio = link * inv
                    ratio_s[i, g] = ratio
                else:
                    inv = 1.0 / excess[b]
                head = reach[b] * inv
                inv_s[i, g] = inv
                head_s[i, g] = head
                corner[b] = head * reach[b] if t == 0 else corner[b] + head * reach[b]
                if t < piece - 1:
                    excess[b] = 1.0 + ratio * excess[b]
                    reach[b] = reach[b] * ratio
                else:
                    blocks.append(((corner[b], head, inv), starts[b], stiff[b]))
        return blocks

    def forward(load, keep, g, fields):
        y = [[None] * fields for _ in range(PIECES)]
        first = [[None] * fields for _ in range(PIECES)]
        final = [[None] * fields for _ in range(PIECES)]
        for t in range(piece):
            for b in range(PIECES):
                i = b * piece + t
                head = head_s[i, g]
                ratio = ratio_s[i - 1, g] if t else None
                for c in range(fields):
                    f = load(c, i)
                    y[b][c] = f + ratio * y[b][c] if t else f
                    keep(c, i, y[b][c])
                    first[b][c] = first[b][c] + head * y[b][c] if t else head * y[b][c]
                    if t == piece - 1:
                        final[b][c] = inv_s[i, g] * y[b][c]
        return first, final

    def backward(spread, kept, put, g):
        for b in range(PIECES):
            now = [None] * len(spread)
            for t in reversed(range(piece)):
                i = b * piece + t
                head = head_s[i, g]
                inv = inv_s[i, g]
                if t < piece - 1:
                    ratio = ratio_s[i, g]
                for f in range(len(spread)):
                    fin, fout = spread[f][b]
                    terms = [times(head, fin)]
                    if kept is not None:
                        terms.append(kept(f, i) * inv)
                    if t < piece - 1:
                        terms.append(ratio * now[f])
                    value = total(terms)
                    if t == piece - 1 and fout is not None:
                        value = value - fout * inv
                    now[f] = value
                    put(f, i, value)

    loads[0].wait()
    parts = []
    for g in range(groups):
        spread_rows(stiff_t.at[g], visc[g * LANES : (g + 1) * LANES, :].T)
        parts.append(factor(stiff_t.at[g], g))
    blocks = [
        (tuple(jnp.stack([p[b][0][q] for p in parts]) for q in range(3)),
         jnp.stack([p[b][1] for p in parts]), jnp.stack([p[b][2] for p in parts]))
        for b in range(PIECES)
    ]
    whole, piece_levels = join_tree(blocks)
    for slot, value in enumerate(whole[0] + whole[1:]):
        put_segments(seg_a, slot, value)
    blocks = []
    for s in range(SEGMENTS):
        v = [take_segment(seg_a, slot, s) for slot in range(5)]
        blocks.append((tuple(v[:3]), v[3], v[4]))
    mine, levels = join_tree(blocks)
    for q, value in enumerate(mine[0] + (mine[1], mine[2])):
        msg_a[q * groups : (q + 1) * groups, :] = value

    each = 2 - second
    beside = jnp.where(has_below, each, 0) + jnp.where(has_above, each, 0)
    pl.semaphore_wait(barrier, devices - 1 + beside)

    def send_rows(side, target):
        @pl.when(is_first)
        def _():
            beside_copy(side, target).start()

        wall_copy(side, target).start()

    @pl.when(has_below)
    def _():
        send_rows(1, wall - 1)

    @pl.when(has_above)
    def _():
        send_rows(0, wall + 1)

    @pl.when(jnp.logical_not(has_below))
    def _():
        got_w[0] = jnp.zeros(got_w.shape[1:], jnp.float32)
        got_s[0] = jnp.zeros(got_w.shape[1:], jnp.float32)

    @pl.when(jnp.logical_not(has_above))
    def _():
        got_w[1] = jnp.zeros(got_w.shape[1:], jnp.float32)
        got_s[1] = jnp.zeros(got_w.shape[1:], jnp.float32)

    for d in range(1, devices):
        ring_copy(d, msg_a, got_a, ring_sem.at[0, 0], ring_sem.at[0, 1]).start()
    zero = jnp.zeros((groups, LANES), jnp.float32)
    unit = jnp.ones((groups, LANES), jnp.float32)

    def solve_fields(chosen):
        for f in chosen:
            if f < components:
                picked = [[j[f] for j in level] for level in jumps]
                flows = down_tree(levels, picked, None, None)
            elif f == components:
                flows = down_tree(levels, None, 1.0, None)
            else:
                flows = down_tree(levels, None, None, 1.0)
            for s, (fin, fout) in enumerate(flows):
                for side, term in enumerate((fin, fout)):
                    term = zero if term is None else unit if isinstance(term, float) else term
                    seg_f[2 * f + side, s * step : s * step + groups, :] = term
        for g in range(groups):
            near = [[tuple(w[g] for w in weights) for weights in level] for level in piece_levels]
            spread = []
            for f in chosen:
                fin, fout = (seg_f[2 * f + side, pl.ds(g, SEGMENTS, stride=step), :] for side in range(2))
                picked = [[j[f][g] for j in level] for level in piece_jumps] if f < components else None
                spread.append(down_tree(near, picked, fin, fout))

            def put(n, i, value, g=g):
                sol_t[chosen[n], g, at_position(i), :] = value

            kept = None if chosen[0] >= components else lambda n, i, g=g: y_s[chosen[n], i, g]
            backward(spread, kept, put, g)
            for f in chosen:
                sol[f, g * LANES : (g + 1) * LANES, :] = gather_rows(sol_t.at[f, g]).T

    solve_fields([components, components + 1])
    ends = [(side, p, p * rows + side * (rows - 1)) for side in range(2) for p in range(planes)]
    for side, p, r in ends:
        for f in range(2):
            e = (f * 2 + side) * planes + p
            msg_c[e : e + 1, :] = sol[components + f, r : r + 1, :]
    @pl.when(is_first)
    def _():
        rows_copy.start()

    row_plane = lax.broadcasted_iota(jnp.int32, (8, 1), 0) % planes

    def by_plane(pick):
        tile = pick(0)
        for p in range(1, planes):
            tile = jnp.where(row_plane == p, pick(p), tile)
        return tile

    def side_rows(source, f, side):
        base = (f * 2 + side) * planes
        return by_plane(lambda p: source[base + p : base + p + 1, :])
    loads[1].wait()
    coef_s[...] = jnp.zeros(coef_s.shape, jnp.float32)
    coef_s[0:2, 0:rows] = coef[...]
    slopes = coef_s[...].T
    await_all(vel.at[:, :, 8 : 8 + rows, :], load_sem.at[2])
    for r in range(0, rows, 8):
        up = jnp.broadcast_to(slopes[r : r + 8, 0:1], (8, LANES))
        down = jnp.broadcast_to(slopes[r : r + 8, 1:2], (8, LANES))
        keep = 1.0 - up - down
        for a in range(slabs):
            c, p = a // planes, a % planes
            for h in range(cells // LANES):
                src[c, p * rows + r : p * rows + r + 8, h * LANES : (h + 1) * LANES] = (
                    keep * vel[h, a, 8 + r : 16 + r, :]
                    + up * vel[h, a, 9 + r : 17 + r, :]
                    + down * vel[h, a, 7 + r : 15 + r, :]
                )
    firsts, finals = [], []
    for g in range(groups):
        for c in range(components):
            spread_rows(src_t.at[c, g], src[c, g * LANES : (g + 1) * LANES, :].T)

        def keep_y(c, i, value, g=g):
            y_s[c, i, g] = value

        first, final = forward(lambda c, i, g=g: src_t[c, g, at_position(i), :], keep_y, g, components)
        firsts.append(first)
        finals.append(final)
    values = [
        ([jnp.stack([v[b][c] for v in firsts]) for c in range(components)],
         [jnp.stack([v[b][c] for v in finals]) for c in range(components)])
        for b in range(PIECES)
    ]
    whole, piece_jumps = value_tree(values, piece_levels)
    for slot, value in enumerate(whole[0] + whole[1]):
        put_segments(seg_b, slot, value)
    values = []
    for s in range(SEGMENTS):
        v = [take_segment(seg_b, slot, s) for slot in range(2 * components)]
        values.append((v[:components], v[components:]))
    own, jumps = value_tree(values, levels)
    for q, value in enumerate(own[0] + own[1]):
        msg_b[q * groups : (q + 1) * groups, :] = value
    for d in range(1, devices):
        ring_copy(d, msg_b, got_b, ring_sem.at[1, 0], ring_sem.at[1, 1]).start()
    @pl.when(is_second)
    def _():
        rows_copy.wait_recv()

        @pl.when(has_below)
        def _():
            await_all(got_w, wall_recv.at[0])

        @pl.when(has_above)
        def _():
            await_all(got_w, wall_recv.at[1])

        lane_kind = lax.broadcasted_iota(jnp.int32, (8, LANES), 1) % 4
        for side in range(2):
            tile = None
            for n, (halo, source) in enumerate(((got_w, msg_c), (got_s, got_c))):
                for f in range(2):
                    value = jnp.sum(halo[side] * side_rows(source, f, side), axis=1, keepdims=True)
                    value = jnp.broadcast_to(value, (8, LANES))
                    tile = value if tile is None else jnp.where(lane_kind == 2 * n + f, value, tile)
            msg_d[side * 8 : side * 8 + 8, :] = tile
        for d in range(1, devices):
            ring_copy(d, msg_d, got_d, ring_sem.at[3, 0], ring_sem.at[3, 1]).start()
    solve_fields(list(range(components)))
    rim[...] = jnp.ones(rim.shape, jnp.float32)
    for side, p, r in ends:
        for c in range(components):
            e = side * 8 + c * planes + p
            rim[e : e + 1, :] = visc[r : r + 1, :]
    spread_rows(rim_t.at[0], rim[...].T)
    whole, rim_piece_levels = join_tree(factor(rim_t.at[0], groups))
    rim_blocks = whole[0] + whole[1:]
    for slot, value in enumerate(rim_blocks):
        seg_a[slot, 0:SEGMENTS, :] = value
    blocks = []
    for s in range(SEGMENTS):
        v = [seg_a[slot, s : s + 1, :] for slot in range(5)]
        blocks.append((tuple(v[:3]), v[3], v[4]))
    _, rim_levels = join_tree(blocks)

    scales = (slopes[0:1, 1:2], slopes[rows - 1 : rows, 0:1])
    await_all(got_a, ring_sem.at[0, 1])
    others = []
    for t in range(1, devices):
        slot = devices - t - 1
        v = [got_a[slot, q * groups : (q + 1) * groups, :] for q in range(5)]
        others.append((tuple(v[:3]), v[3], v[4]))
    rest, ring_levels = join_tree(others)
    (m00, m0l, mll), m_first, m_last = mine
    (b00, b0l, bll), b_first, b_last = rest
    out_diag = 2.0 / (m_last + b_first) + mll + b00
    in_diag = 2.0 / (b_last + m_first) + bll + m00
    cross = m0l + b0l
    det = 1.0 / (out_diag * in_diag - cross * cross)
    near_in, near_out, across = out_diag * det, in_diag * det, cross * det

    def put_weights(leaf, weights):
        for way in range(2):
            for f in range(2):
                for n in range(2):
                    k = 4 * ((leaf - n) % devices) + 2 * n + f
                    for g in range(groups):
                        weigh[way, g, k : k + 1, :] = weights[way][f][g : g + 1]

    put_weights(0, ((0.0 - near_in, 0.0 - across), (0.0 - across, 0.0 - near_out)))
    to_first = down_tree(ring_levels, None, 1.0, None)
    to_last = down_tree(ring_levels, None, None, 1.0)
    for t in range(1, devices):
        pairs = list(zip(to_first[t - 1], to_last[t - 1]))
        put_weights(devices - t, [
            [0.0 - total((times(by_first, from_first), times(by_last, from_last))) for from_first, from_last in pairs]
            for by_first, by_last in ((across, near_in), (near_out, across))
        ])
    tables = {}
    for way in range(2):
        turned = [weigh[way, g].T for g in range(groups)]
        for side in range(2):
            def pick(p):
                r = p * rows + side * (rows - 1)
                line = r % LANES
                return turned[r // LANES][line : line + 1, :]
            tables[side, way] = by_plane(pick) * scales[side]

    @pl.when(jnp.logical_and(is_first, has_below))
    def _():
        wall_copy(0, wall).wait_recv()

    @pl.when(jnp.logical_and(is_first, has_above))
    def _():
        wall_copy(1, wall).wait_recv()

    for side in range(2):
        rim[side * 8 : side * 8 + 8, :] = got_w[side] * scales[side]
    spread_rows(rim_t.at[0], rim[...].T)
    held = {}

    def keep_rim(c, i, value):
        held[i] = value

    first, final = forward(lambda c, i: rim_t[0, at_position(i), :], keep_rim, groups, 1)
    whole, rim_piece_jumps = value_tree([(first[b], final[b]) for b in range(PIECES)], rim_piece_levels)
    seg_b[0, 0:SEGMENTS, :] = whole[0][0]
    seg_b[1, 0:SEGMENTS, :] = whole[1][0]
    _, rim_jumps = value_tree(
        [([seg_b[0, s : s + 1, :]], [seg_b[1, s : s + 1, :]]) for s in range(SEGMENTS)], rim_levels)
    picked = [[j[0] for j in level] for level in rim_jumps]
    for s, terms in enumerate(down_tree(rim_levels, picked, None, None)):
        for side, term in enumerate(terms):
            term = jnp.zeros((1, LANES), jnp.float32) if term is None else term
            seg_f[side, s : s + 1, :] = term
    picked = [[j[0] for j in level] for level in rim_piece_jumps]
    spread = [down_tree(rim_piece_levels, picked, seg_f[0, 0:SEGMENTS, :], seg_f[1, 0:SEGMENTS, :])]

    def put_rim(n, i, value):
        rim_t[1, at_position(i), :] = value

    backward(spread, lambda n, i: held[i], put_rim, groups)
    rim_sol[...] = gather_rows(rim_t.at[1]).T
    await_all(got_b, ring_sem.at[1, 1])
    theirs = []
    for t in range(1, devices):
        slot = devices - t - 1
        v = [got_b[slot, q * groups : (q + 1) * groups, :] for q in range(2 * components)]
        theirs.append((v[:components], v[components:]))
    tail, _ = value_tree(theirs, ring_levels)
    for c in range(components):
        gap_out = own[1][c] - tail[0][c]
        gap_in = tail[1][c] - own[0][c]
        outflow = near_out * gap_out + across * gap_in
        inflow = near_in * gap_in + across * gap_out
        for g in range(groups):
            flow[g, c : c + 1, :] = inflow[g : g + 1]
            flow[g, components + c : components + c + 1, :] = outflow[g : g + 1]

    for g in range(groups):
        span = slice(g * LANES, (g + 1) * LANES)
        columns = flow[g].T
        from_left = sol[components, span, :]
        from_right = sol[components + 1, span, :]
        for c in range(components):
            out[c, span, :] = (
                sol[c, span, :]
                + columns[:, c : c + 1] * from_left
                + columns[:, components + c : components + c + 1] * from_right
            )
    for n, sent in enumerate((got_a, got_b)):
        await_all(sent, ring_sem.at[n, 0])

    @pl.when(is_first)
    def _():
        rows_copy.wait_send()

        @pl.when(has_above)
        def _():
            await_all(got_w, wall_send.at[0])

        @pl.when(has_below)
        def _():
            await_all(got_w, wall_send.at[1])

        await_all(got_d.at[0 : devices // 2], ring_sem.at[3, 1])

    @pl.when(is_second)
    def _():
        @pl.when(has_above)
        def _():
            await_all(got_w.at[0], wall_send.at[0])

        @pl.when(has_below)
        def _():
            await_all(got_w.at[1], wall_send.at[1])

        await_all(got_d, ring_sem.at[3, 0])
        await_all(got_d.at[0 : devices // 2 - 1], ring_sem.at[3, 1])

    lane_slot = lax.broadcasted_iota(jnp.int32, (8, 4 * devices), 1) // 4
    for side in range(2):
        held_rows = slice(side * 8, side * 8 + 8)
        mix = jnp.where(is_second, msg_d[held_rows, 0 : 4 * devices], 0.0)
        for d in range(1, devices):
            mix = jnp.where(lane_slot == d, got_d[d - 1, held_rows, 0 : 4 * devices], mix)
        ways = [jnp.sum(mix * tables[side, way], axis=1, keepdims=True) for way in range(2)]
        added = (
            rim_sol[side * 8 : side * 8 + 8, :] + ways[0] * side_rows(msg_c, 0, side) + ways[1] * side_rows(msg_c, 1, side)
        )
        for c in range(components):
            for p in range(planes):
                r = p * rows + side * (rows - 1)
                e = c * planes + p
                out[c, r : r + 1, :] = out[c, r : r + 1, :] + added[e : e + 1, :]


def shards(devices, wall_devices, velocity, viscosity, y_coef):
    components, planes, rows, cells = velocity.shape
    lines = planes * rows
    slabs = components * planes
    groups = lines // LANES
    length = cells // SEGMENTS
    fields = components + 2
    f32 = jnp.float32
    rows_a, rows_b, rows_c = up8(5 * groups), up8(2 * components * groups), up8(4 * planes)
    peers = devices - 1
    sweeps = (length, groups + 1, SEGMENTS, LANES)
    turned = (SEGMENTS * odd(length), LANES)
    joints = SEGMENTS * odd(groups)
    vmem = pl.BlockSpec(memory_space=pltpu.VMEM)
    result = pl.pallas_call(
        functools.partial(kernel, devices, wall_devices, planes),
        out_shape=jax.ShapeDtypeStruct((components, lines, cells), f32),
        in_specs=[pl.BlockSpec(memory_space=pltpu.HBM)] * 3,
        out_specs=vmem,
        scratch_shapes=[
            pltpu.VMEM((cells // LANES, slabs, rows + 16, LANES), f32),
            pltpu.VMEM((lines, cells), f32),
            pltpu.VMEM(y_coef.shape, f32),
            pltpu.VMEM((2, slabs, 8, cells), f32),
            pltpu.VMEM((2, 8, cells), f32),
            pltpu.VMEM((2, 8, cells), f32),
            pltpu.VMEM((2, 8, cells), f32),
            pltpu.VMEM((groups,) + turned, f32),
            pltpu.VMEM((components, lines, cells), f32),
            pltpu.VMEM((components, groups) + turned, f32),
            pltpu.VMEM(sweeps, f32),
            pltpu.VMEM(sweeps, f32),
            pltpu.VMEM(sweeps, f32),
            pltpu.VMEM((components, length, groups, SEGMENTS, LANES), f32),
            pltpu.VMEM((5, joints, LANES), f32),
            pltpu.VMEM((2 * components, joints, LANES), f32),
            pltpu.VMEM((2 * fields, joints, LANES), f32),
            pltpu.VMEM((groups, up8(2 * components), LANES), f32),
            pltpu.VMEM((fields, groups) + turned, f32),
            pltpu.VMEM((fields, lines, cells), f32),
            pltpu.VMEM((LANES, cells), f32),
            pltpu.VMEM((2,) + turned, f32),
            pltpu.VMEM((LANES, cells), f32),
            pltpu.VMEM((2, groups, 4 * devices, LANES), f32),
            pltpu.VMEM((8, -(-rows // LANES) * LANES), f32),
            pltpu.VMEM((rows_a, LANES), f32),
            pltpu.VMEM((rows_b, LANES), f32),
            pltpu.VMEM((rows_c, cells), f32),
            pltpu.VMEM((16, LANES), f32),
            pltpu.VMEM((peers, rows_a, LANES), f32),
            pltpu.VMEM((peers, rows_b, LANES), f32),
            pltpu.VMEM((rows_c, cells), f32),
            pltpu.VMEM((peers, 16, LANES), f32),
            pltpu.SemaphoreType.DMA((4,)),
            pltpu.SemaphoreType.DMA((2,)),
            pltpu.SemaphoreType.DMA((2,)),
            pltpu.SemaphoreType.DMA((4, 2)),
        ],
        compiler_params=pltpu.CompilerParams(
            collective_id=0, has_side_effects=True, vmem_limit_bytes=40 * 1024 * 1024
        ),
        name="implicit_lines",
    )(
        pltpu.with_memory_space_constraint(velocity.reshape(slabs, rows, cells), pltpu.HBM),
        pltpu.with_memory_space_constraint(viscosity.reshape(lines, cells), pltpu.HBM),
        pltpu.with_memory_space_constraint(y_coef, pltpu.HBM),
    )
    return result.reshape(velocity.shape)


def solution(mesh):
    placed = (P(None, None, "wall", "stream"), P(None, "wall", "stream"), P(None, "wall"))
    return jax.shard_map(
        functools.partial(shards, mesh.shape["stream"], mesh.shape["wall"]),
        mesh=mesh,
        in_specs=placed,
        out_specs=P(None, None, "wall", "stream"),
        check_vma=False,
    )
```

```python
import functools

import jax
import jax.numpy as jnp
from jax import lax
from jax.experimental import pallas as pl
from jax.experimental.pallas import tpu as pltpu
from jax.sharding import PartitionSpec as P

SEGMENTS = 8
PIECES = 4
LANES = 128
MESH = pl.DeviceIdType.MESH


def up8(rows):
    return -(-rows // 8) * 8


def join_matrix(a, b, link):
    a00, a0l, all_ = a
    b00, b0l, bll = b
    gain = link / (1.0 + link * (all_ + b00))
    left = gain * a0l
    right = gain * b0l
    return (a00 - left * a0l, left * b0l, bll - right * b0l), (gain, left, right)


def join_values(a, b, weights):
    _, left, right = weights
    jump = [al - b0 for al, b0 in zip(a[1], b[0])]
    first = [a0 - left * j for a0, j in zip(a[0], jump)]
    last = [bl + right * j for bl, j in zip(b[1], jump)]
    return (first, last), jump


def join_tree(blocks):
    levels = []
    while len(blocks) > 1:
        merged, weights = [], []
        for i in range(0, len(blocks) - 1, 2):
            (ma, fa, la), (mb, fb, lb) = blocks[i], blocks[i + 1]
            m, w = join_matrix(ma, mb, 0.5 * (la + fb))
            merged.append((m, fa, lb))
            weights.append(w)
        if len(blocks) % 2:
            merged.append(blocks[-1])
        levels.append(weights)
        blocks = merged
    return blocks[0], levels


def value_tree(values, levels):
    jumps = []
    for weights in levels:
        merged, jump = [], []
        for i, w in enumerate(weights):
            v, j = join_values(values[2 * i], values[2 * i + 1], w)
            merged.append(v)
            jump.append(j)
        if len(values) % 2:
            merged.append(values[-1])
        jumps.append(jump)
        values = merged
    return values[0], jumps


def down_tree(levels, jumps, inflow, outflow):
    flows = [(inflow, outflow)]
    for depth in reversed(range(len(levels))):
        spread = []
        for i, (gain, left, right) in enumerate(levels[depth]):
            fin, fout = flows[i]
            middle = None
            for term, weight in ((fin, left), (fout, right)):
                if term is not None:
                    part = weight if isinstance(term, float) else term * weight
                    middle = part if middle is None else middle + part
            if jumps is not None:
                part = gain * jumps[depth][i]
                middle = part if middle is None else middle + part
            spread += [(fin, middle), (middle, fout)]
        flows = spread + flows[len(levels[depth]) :]
    return flows


def odd(rows):
    return rows | 1


def total(terms):
    result = None
    for term in terms:
        if term is not None:
            result = term if result is None else result + term
    return result


def times(weight, flow):
    return None if flow is None else weight if isinstance(flow, float) else weight * flow


def kernel(devices, wall_devices, planes, vel_hbm, visc_hbm, coef_hbm, out,
           vel, visc, coef, edge, wall_out, got_w, got_s, stiff_t, src, src_t, ratio_s, inv_s, head_s, y_s, seg_a, seg_b,
           seg_f, flow, sol_t, sol, rim, rim_t, rim_sol, weigh, coef_s, msg_a, msg_b, msg_c, msg_d, got_a, got_b, got_c, got_d,
           load_sem, wall_send, wall_recv, ring_sem):
    slabs, rows, cells = vel_hbm.shape
    components = slabs // planes
    lines = planes * rows
    groups = lines // LANES
    length = cells // SEGMENTS
    piece = length // PIECES
    pitch = odd(length)
    step = odd(groups)
    me = lax.axis_index("stream")
    wall = lax.axis_index("wall")
    has_below = wall > 0
    has_above = wall < wall_devices - 1
    second = lax.rem(me, 2)
    is_first, is_second = second == 0, second == 1
    barrier = pltpu.get_barrier_semaphore()
    edges = [
        pltpu.make_async_copy(vel_hbm.at[:, rows - 8 : rows, :], edge.at[0], load_sem.at[3]),
        pltpu.make_async_copy(vel_hbm.at[:, 0:8, :], edge.at[1], load_sem.at[3]),
    ]
    loads = [
        pltpu.make_async_copy(visc_hbm, visc, load_sem.at[0]),
        pltpu.make_async_copy(coef_hbm, coef, load_sem.at[1]),
    ] + [
        pltpu.make_async_copy(
            vel_hbm.at[:, :, h * LANES : (h + 1) * LANES], vel.at[h, :, 8 : 8 + rows, :], load_sem.at[2])
        for h in range(cells // LANES)
    ]
    def await_all(landed, sem):
        pltpu.make_async_copy(landed, landed, sem).wait()

    def around(d):
        return lax.rem(me + d, devices)

    def greet(target):
        pl.semaphore_signal(barrier, inc=1, device_id={"wall": target}, device_id_type=MESH)

        @pl.when(is_second)
        def _():
            pl.semaphore_signal(
                barrier, inc=1, device_id={"wall": target, "stream": me - 1}, device_id_type=MESH)

    got_d[...] = jnp.zeros(got_d.shape, jnp.float32)
    got_w[:, slabs:8, :] = jnp.zeros((2, 8 - slabs, cells), jnp.float32)
    got_s[:, slabs:8, :] = jnp.zeros((2, 8 - slabs, cells), jnp.float32)
    msg_d[...] = jnp.zeros(msg_d.shape, jnp.float32)

    @pl.when(has_below)
    def _():
        greet(wall - 1)

    @pl.when(has_above)
    def _():
        greet(wall + 1)

    for d in sorted(range(1, devices), key=lambda d: -min(d, devices - d)):
        pl.semaphore_signal(barrier, inc=1, device_id={"stream": around(d)}, device_id_type=MESH)

    for load in edges + loads:
        load.start()

    nothing = jnp.zeros((cells // LANES, slabs, 1, LANES), jnp.float32)
    vel[:, :, 7:8, :] = nothing
    vel[:, :, 8 + rows : 9 + rows, :] = nothing
    wall_out[...] = jnp.zeros(wall_out.shape, jnp.float32)
    await_all(edge, load_sem.at[3])
    for a in range(slabs):
        wall_out[0, a : a + 1, :] = edge[0, a, 7:8, :]
        wall_out[1, a : a + 1, :] = edge[1, a, 0:1, :]

    def wall_copy(side, target):
        return pltpu.make_async_remote_copy(
            src_ref=wall_out.at[side, 0:slabs], dst_ref=got_w.at[side, 0:slabs],
            send_sem=wall_send.at[side], recv_sem=wall_recv.at[side],
            device_id={"wall": target}, device_id_type=MESH)

    def beside_copy(side, target):
        return pltpu.make_async_remote_copy(
            src_ref=wall_out.at[side, 0:slabs], dst_ref=got_s.at[side, 0:slabs],
            send_sem=wall_send.at[side], recv_sem=wall_recv.at[side],
            device_id={"wall": target, "stream": me + 1 - 2 * second}, device_id_type=MESH)

    rows_copy = pltpu.make_async_remote_copy(
        src_ref=msg_c, dst_ref=got_c, send_sem=ring_sem.at[2, 0], recv_sem=ring_sem.at[2, 1],
        device_id={"stream": me + 1 - 2 * second}, device_id_type=MESH)

    def ring_copy(d, source, target, send, recv):
        return pltpu.make_async_remote_copy(
            src_ref=source, dst_ref=target.at[d - 1],
            send_sem=send, recv_sem=recv,
            device_id={"stream": around(d)}, device_id_type=MESH)

    def at_position(i):
        return pl.ds(i, SEGMENTS, stride=pitch)

    def put_segments(buffer, slot, value):
        for g in range(groups):
            buffer[slot, pl.ds(g, SEGMENTS, stride=step), :] = value[g]

    def take_segment(buffer, slot, s):
        return buffer[slot, s * step : s * step + groups, :]

    def spread_rows(target, turned):
        for s in range(SEGMENTS):
            target[s * pitch : s * pitch + length, :] = turned[s * length : (s + 1) * length, :]

    def gather_rows(source):
        return jnp.concatenate([source[s * pitch : s * pitch + length, :] for s in range(SEGMENTS)])

    def factor(source, g):
        one = jnp.ones((SEGMENTS, LANES), jnp.float32)
        excess, reach = [one] * PIECES, [one] * PIECES
        corner = [None] * PIECES
        stiff = [source[at_position(b * piece), :] for b in range(PIECES)]
        starts = list(stiff)
        blocks = []
        for t in range(piece):
            for b in range(PIECES):
                i = b * piece + t
                if t < piece - 1:
                    following = source[at_position(i + 1), :]
                    link = 0.5 * (stiff[b] + following)
                    stiff[b] = following
                    inv = 1.0 / (excess[b] + link)
                    ratio = link * inv
                    ratio_s[i, g] = ratio
                else:
                    inv = 1.0 / excess[b]
                head = reach[b] * inv
                inv_s[i, g] = inv
                head_s[i, g] = head
                corner[b] = head * reach[b] if t == 0 else corner[b] + head * reach[b]
                if t < piece - 1:
                    excess[b] = 1.0 + ratio * excess[b]
                    reach[b] = reach[b] * ratio
                else:
                    blocks.append(((corner[b], head, inv), starts[b], stiff[b]))
        return blocks

    def forward(load, keep, g, fields):
        y = [[None] * fields for _ in range(PIECES)]
        first = [[None] * fields for _ in range(PIECES)]
        final = [[None] * fields for _ in range(PIECES)]
        for t in range(piece):
            for b in range(PIECES):
                i = b * piece + t
                head = head_s[i, g]
                ratio = ratio_s[i - 1, g] if t else None
                for c in range(fields):
                    f = load(c, i)
                    y[b][c] = f + ratio * y[b][c] if t else f
                    keep(c, i, y[b][c])
                    first[b][c] = first[b][c] + head * y[b][c] if t else head * y[b][c]
                    if t == piece - 1:
                        final[b][c] = inv_s[i, g] * y[b][c]
        return first, final

    def backward(spread, kept, put, g):
        for b in range(PIECES):
            now = [None] * len(spread)
            for t in reversed(range(piece)):
                i = b * piece + t
                head = head_s[i, g]
                inv = inv_s[i, g]
                if t < piece - 1:
                    ratio = ratio_s[i, g]
                for f in range(len(spread)):
                    fin, fout = spread[f][b]
                    terms = [times(head, fin)]
                    if kept is not None:
                        terms.append(kept(f, i) * inv)
                    if t < piece - 1:
                        terms.append(ratio * now[f])
                    value = total(terms)
                    if t == piece - 1 and fout is not None:
                        value = value - fout * inv
                    now[f] = value
                    put(f, i, value)

    loads[0].wait()
    parts = []
    for g in range(groups):
        spread_rows(stiff_t.at[g], visc[g * LANES : (g + 1) * LANES, :].T)
        parts.append(factor(stiff_t.at[g], g))
    blocks = [
        (tuple(jnp.stack([p[b][0][q] for p in parts]) for q in range(3)),
         jnp.stack([p[b][1] for p in parts]), jnp.stack([p[b][2] for p in parts]))
        for b in range(PIECES)
    ]
    whole, piece_levels = join_tree(blocks)
    for slot, value in enumerate(whole[0] + whole[1:]):
        put_segments(seg_a, slot, value)
    blocks = []
    for s in range(SEGMENTS):
        v = [take_segment(seg_a, slot, s) for slot in range(5)]
        blocks.append((tuple(v[:3]), v[3], v[4]))
    mine, levels = join_tree(blocks)
    for q, value in enumerate(mine[0] + (mine[1], mine[2])):
        msg_a[q * groups : (q + 1) * groups, :] = value

    each = 2 - second
    beside = jnp.where(has_below, each, 0) + jnp.where(has_above, each, 0)
    pl.semaphore_wait(barrier, devices - 1 + beside)

    def send_rows(side, target):
        @pl.when(is_first)
        def _():
            beside_copy(side, target).start()

        wall_copy(side, target).start()

    @pl.when(has_below)
    def _():
        send_rows(1, wall - 1)

    @pl.when(has_above)
    def _():
        send_rows(0, wall + 1)

    @pl.when(jnp.logical_not(has_below))
    def _():
        got_w[0] = jnp.zeros(got_w.shape[1:], jnp.float32)
        got_s[0] = jnp.zeros(got_w.shape[1:], jnp.float32)

    @pl.when(jnp.logical_not(has_above))
    def _():
        got_w[1] = jnp.zeros(got_w.shape[1:], jnp.float32)
        got_s[1] = jnp.zeros(got_w.shape[1:], jnp.float32)

    for d in range(1, devices):
        ring_copy(d, msg_a, got_a, ring_sem.at[0, 0], ring_sem.at[0, 1]).start()
    zero = jnp.zeros((groups, LANES), jnp.float32)
    unit = jnp.ones((groups, LANES), jnp.float32)

    def solve_fields(chosen):
        for f in chosen:
            if f < components:
                picked = [[j[f] for j in level] for level in jumps]
                flows = down_tree(levels, picked, None, None)
            elif f == components:
                flows = down_tree(levels, None, 1.0, None)
            else:
                flows = down_tree(levels, None, None, 1.0)
            for s, (fin, fout) in enumerate(flows):
                for side, term in enumerate((fin, fout)):
                    term = zero if term is None else unit if isinstance(term, float) else term
                    seg_f[2 * f + side, s * step : s * step + groups, :] = term
        for g in range(groups):
            near = [[tuple(w[g] for w in weights) for weights in level] for level in piece_levels]
            spread = []
            for f in chosen:
                fin, fout = (seg_f[2 * f + side, pl.ds(g, SEGMENTS, stride=step), :] for side in range(2))
                picked = [[j[f][g] for j in level] for level in piece_jumps] if f < components else None
                spread.append(down_tree(near, picked, fin, fout))

            def put(n, i, value, g=g):
                sol_t[chosen[n], g, at_position(i), :] = value

            kept = None if chosen[0] >= components else lambda n, i, g=g: y_s[chosen[n], i, g]
            backward(spread, kept, put, g)
            for f in chosen:
                sol[f, g * LANES : (g + 1) * LANES, :] = gather_rows(sol_t.at[f, g]).T

    solve_fields([components, components + 1])
    ends = [(side, p, p * rows + side * (rows - 1)) for side in range(2) for p in range(planes)]
    for side, p, r in ends:
        for f in range(2):
            e = (f * 2 + side) * planes + p
            msg_c[e : e + 1, :] = sol[components + f, r : r + 1, :]
    @pl.when(is_first)
    def _():
        rows_copy.start()

    row_plane = lax.broadcasted_iota(jnp.int32, (8, 1), 0) % planes

    def by_plane(pick):
        tile = pick(0)
        for p in range(1, planes):
            tile = jnp.where(row_plane == p, pick(p), tile)
        return tile

    def side_rows(source, f, side):
        base = (f * 2 + side) * planes
        return by_plane(lambda p: source[base + p : base + p + 1, :])
    loads[1].wait()
    coef_s[...] = jnp.zeros(coef_s.shape, jnp.float32)
    coef_s[0:2, 0:rows] = coef[...]
    slopes = coef_s[...].T
    await_all(vel.at[:, :, 8 : 8 + rows, :], load_sem.at[2])
    for r in range(0, rows, 8):
        up = jnp.broadcast_to(slopes[r : r + 8, 0:1], (8, LANES))
        down = jnp.broadcast_to(slopes[r : r + 8, 1:2], (8, LANES))
        keep = 1.0 - up - down
        for a in range(slabs):
            c, p = a // planes, a % planes
            for h in range(cells // LANES):
                src[c, p * rows + r : p * rows + r + 8, h * LANES : (h + 1) * LANES] = (
                    keep * vel[h, a, 8 + r : 16 + r, :]
                    + up * vel[h, a, 9 + r : 17 + r, :]
                    + down * vel[h, a, 7 + r : 15 + r, :]
                )
    firsts, finals = [], []
    for g in range(groups):
        for c in range(components):
            spread_rows(src_t.at[c, g], src[c, g * LANES : (g + 1) * LANES, :].T)

        def keep_y(c, i, value, g=g):
            y_s[c, i, g] = value

        first, final = forward(lambda c, i, g=g: src_t[c, g, at_position(i), :], keep_y, g, components)
        firsts.append(first)
        finals.append(final)
    values = [
        ([jnp.stack([v[b][c] for v in firsts]) for c in range(components)],
         [jnp.stack([v[b][c] for v in finals]) for c in range(components)])
        for b in range(PIECES)
    ]
    whole, piece_jumps = value_tree(values, piece_levels)
    for slot, value in enumerate(whole[0] + whole[1]):
        put_segments(seg_b, slot, value)
    values = []
    for s in range(SEGMENTS):
        v = [take_segment(seg_b, slot, s) for slot in range(2 * components)]
        values.append((v[:components], v[components:]))
    own, jumps = value_tree(values, levels)
    for q, value in enumerate(own[0] + own[1]):
        msg_b[q * groups : (q + 1) * groups, :] = value
    for d in range(1, devices):
        ring_copy(d, msg_b, got_b, ring_sem.at[1, 0], ring_sem.at[1, 1]).start()
    @pl.when(is_second)
    def _():
        rows_copy.wait_recv()

        @pl.when(has_below)
        def _():
            await_all(got_w.at[:, 0:slabs], wall_recv.at[0])

        @pl.when(has_above)
        def _():
            await_all(got_w.at[:, 0:slabs], wall_recv.at[1])

        lane_kind = lax.broadcasted_iota(jnp.int32, (8, LANES), 1) % 4
        for side in range(2):
            tile = None
            for n, (halo, source) in enumerate(((got_w, msg_c), (got_s, got_c))):
                for f in range(2):
                    value = jnp.sum(halo[side] * side_rows(source, f, side), axis=1, keepdims=True)
                    value = jnp.broadcast_to(value, (8, LANES))
                    tile = value if tile is None else jnp.where(lane_kind == 2 * n + f, value, tile)
            msg_d[side * 8 : side * 8 + 8, :] = tile
        for d in range(1, devices):
            ring_copy(d, msg_d, got_d, ring_sem.at[3, 0], ring_sem.at[3, 1]).start()
    solve_fields(list(range(components)))
    rim[...] = jnp.ones(rim.shape, jnp.float32)
    for side, p, r in ends:
        for c in range(components):
            e = side * 8 + c * planes + p
            rim[e : e + 1, :] = visc[r : r + 1, :]
    spread_rows(rim_t.at[0], rim[...].T)
    whole, rim_piece_levels = join_tree(factor(rim_t.at[0], groups))
    rim_blocks = whole[0] + whole[1:]
    for slot, value in enumerate(rim_blocks):
        seg_a[slot, 0:SEGMENTS, :] = value
    blocks = []
    for s in range(SEGMENTS):
        v = [seg_a[slot, s : s + 1, :] for slot in range(5)]
        blocks.append((tuple(v[:3]), v[3], v[4]))
    _, rim_levels = join_tree(blocks)

    scales = (slopes[0:1, 1:2], slopes[rows - 1 : rows, 0:1])
    await_all(got_a, ring_sem.at[0, 1])
    others = []
    for t in range(1, devices):
        slot = devices - t - 1
        v = [got_a[slot, q * groups : (q + 1) * groups, :] for q in range(5)]
        others.append((tuple(v[:3]), v[3], v[4]))
    rest, ring_levels = join_tree(others)
    (m00, m0l, mll), m_first, m_last = mine
    (b00, b0l, bll), b_first, b_last = rest
    out_diag = 2.0 / (m_last + b_first) + mll + b00
    in_diag = 2.0 / (b_last + m_first) + bll + m00
    cross = m0l + b0l
    det = 1.0 / (out_diag * in_diag - cross * cross)
    near_in, near_out, across = out_diag * det, in_diag * det, cross * det

    def put_weights(leaf, weights):
        for way in range(2):
            for f in range(2):
                for n in range(2):
                    k = 4 * ((leaf - n) % devices) + 2 * n + f
                    for g in range(groups):
                        weigh[way, g, k : k + 1, :] = weights[way][f][g : g + 1]

    put_weights(0, ((0.0 - near_in, 0.0 - across), (0.0 - across, 0.0 - near_out)))
    to_first = down_tree(ring_levels, None, 1.0, None)
    to_last = down_tree(ring_levels, None, None, 1.0)
    for t in range(1, devices):
        pairs = list(zip(to_first[t - 1], to_last[t - 1]))
        put_weights(devices - t, [
            [0.0 - total((times(by_first, from_first), times(by_last, from_last))) for from_first, from_last in pairs]
            for by_first, by_last in ((across, near_in), (near_out, across))
        ])
    tables = {}
    for way in range(2):
        turned = [weigh[way, g].T for g in range(groups)]
        for side in range(2):
            def pick(p):
                r = p * rows + side * (rows - 1)
                line = r % LANES
                return turned[r // LANES][line : line + 1, :]
            tables[side, way] = by_plane(pick) * scales[side]

    @pl.when(jnp.logical_and(is_first, has_below))
    def _():
        wall_copy(0, wall).wait_recv()

    @pl.when(jnp.logical_and(is_first, has_above))
    def _():
        wall_copy(1, wall).wait_recv()

    for side in range(2):
        rim[side * 8 : side * 8 + 8, :] = got_w[side] * scales[side]
    spread_rows(rim_t.at[0], rim[...].T)
    held = {}

    def keep_rim(c, i, value):
        held[i] = value

    first, final = forward(lambda c, i: rim_t[0, at_position(i), :], keep_rim, groups, 1)
    whole, rim_piece_jumps = value_tree([(first[b], final[b]) for b in range(PIECES)], rim_piece_levels)
    seg_b[0, 0:SEGMENTS, :] = whole[0][0]
    seg_b[1, 0:SEGMENTS, :] = whole[1][0]
    _, rim_jumps = value_tree(
        [([seg_b[0, s : s + 1, :]], [seg_b[1, s : s + 1, :]]) for s in range(SEGMENTS)], rim_levels)
    picked = [[j[0] for j in level] for level in rim_jumps]
    for s, terms in enumerate(down_tree(rim_levels, picked, None, None)):
        for side, term in enumerate(terms):
            term = jnp.zeros((1, LANES), jnp.float32) if term is None else term
            seg_f[side, s : s + 1, :] = term
    picked = [[j[0] for j in level] for level in rim_piece_jumps]
    spread = [down_tree(rim_piece_levels, picked, seg_f[0, 0:SEGMENTS, :], seg_f[1, 0:SEGMENTS, :])]

    def put_rim(n, i, value):
        rim_t[1, at_position(i), :] = value

    backward(spread, lambda n, i: held[i], put_rim, groups)
    rim_sol[...] = gather_rows(rim_t.at[1]).T
    await_all(got_b, ring_sem.at[1, 1])
    theirs = []
    for t in range(1, devices):
        slot = devices - t - 1
        v = [got_b[slot, q * groups : (q + 1) * groups, :] for q in range(2 * components)]
        theirs.append((v[:components], v[components:]))
    tail, _ = value_tree(theirs, ring_levels)
    for c in range(components):
        gap_out = own[1][c] - tail[0][c]
        gap_in = tail[1][c] - own[0][c]
        outflow = near_out * gap_out + across * gap_in
        inflow = near_in * gap_in + across * gap_out
        for g in range(groups):
            flow[g, c : c + 1, :] = inflow[g : g + 1]
            flow[g, components + c : components + c + 1, :] = outflow[g : g + 1]

    for g in range(groups):
        span = slice(g * LANES, (g + 1) * LANES)
        columns = flow[g].T
        from_left = sol[components, span, :]
        from_right = sol[components + 1, span, :]
        for c in range(components):
            out[c, span, :] = (
                sol[c, span, :]
                + columns[:, c : c + 1] * from_left
                + columns[:, components + c : components + c + 1] * from_right
            )
    for n, sent in enumerate((got_a, got_b)):
        await_all(sent, ring_sem.at[n, 0])

    @pl.when(is_first)
    def _():
        rows_copy.wait_send()

        @pl.when(has_above)
        def _():
            await_all(got_w.at[:, 0:slabs], wall_send.at[0])

        @pl.when(has_below)
        def _():
            await_all(got_w.at[:, 0:slabs], wall_send.at[1])

        await_all(got_d.at[0 : devices // 2], ring_sem.at[3, 1])

    @pl.when(is_second)
    def _():
        @pl.when(has_above)
        def _():
            await_all(got_w.at[0, 0:slabs], wall_send.at[0])

        @pl.when(has_below)
        def _():
            await_all(got_w.at[1, 0:slabs], wall_send.at[1])

        await_all(got_d, ring_sem.at[3, 0])
        await_all(got_d.at[0 : devices // 2 - 1], ring_sem.at[3, 1])

    lane_slot = lax.broadcasted_iota(jnp.int32, (8, 4 * devices), 1) // 4
    for side in range(2):
        held_rows = slice(side * 8, side * 8 + 8)
        mix = jnp.where(is_second, msg_d[held_rows, 0 : 4 * devices], 0.0)
        for d in range(1, devices):
            mix = jnp.where(lane_slot == d, got_d[d - 1, held_rows, 0 : 4 * devices], mix)
        ways = [jnp.sum(mix * tables[side, way], axis=1, keepdims=True) for way in range(2)]
        added = (
            rim_sol[side * 8 : side * 8 + 8, :] + ways[0] * side_rows(msg_c, 0, side) + ways[1] * side_rows(msg_c, 1, side)
        )
        for c in range(components):
            for p in range(planes):
                r = p * rows + side * (rows - 1)
                e = c * planes + p
                out[c, r : r + 1, :] = out[c, r : r + 1, :] + added[e : e + 1, :]


def shards(devices, wall_devices, velocity, viscosity, y_coef):
    components, planes, rows, cells = velocity.shape
    lines = planes * rows
    slabs = components * planes
    groups = lines // LANES
    length = cells // SEGMENTS
    fields = components + 2
    f32 = jnp.float32
    rows_a, rows_b, rows_c = up8(5 * groups), up8(2 * components * groups), up8(4 * planes)
    peers = devices - 1
    sweeps = (length, groups + 1, SEGMENTS, LANES)
    turned = (SEGMENTS * odd(length), LANES)
    joints = SEGMENTS * odd(groups)
    vmem = pl.BlockSpec(memory_space=pltpu.VMEM)
    result = pl.pallas_call(
        functools.partial(kernel, devices, wall_devices, planes),
        out_shape=jax.ShapeDtypeStruct((components, lines, cells), f32),
        in_specs=[pl.BlockSpec(memory_space=pltpu.HBM)] * 3,
        out_specs=vmem,
        scratch_shapes=[
            pltpu.VMEM((cells // LANES, slabs, rows + 16, LANES), f32),
            pltpu.VMEM((lines, cells), f32),
            pltpu.VMEM(y_coef.shape, f32),
            pltpu.VMEM((2, slabs, 8, cells), f32),
            pltpu.VMEM((2, 8, cells), f32),
            pltpu.VMEM((2, 8, cells), f32),
            pltpu.VMEM((2, 8, cells), f32),
            pltpu.VMEM((groups,) + turned, f32),
            pltpu.VMEM((components, lines, cells), f32),
            pltpu.VMEM((components, groups) + turned, f32),
            pltpu.VMEM(sweeps, f32),
            pltpu.VMEM(sweeps, f32),
            pltpu.VMEM(sweeps, f32),
            pltpu.VMEM((components, length, groups, SEGMENTS, LANES), f32),
            pltpu.VMEM((5, joints, LANES), f32),
            pltpu.VMEM((2 * components, joints, LANES), f32),
            pltpu.VMEM((2 * fields, joints, LANES), f32),
            pltpu.VMEM((groups, up8(2 * components), LANES), f32),
            pltpu.VMEM((fields, groups) + turned, f32),
            pltpu.VMEM((fields, lines, cells), f32),
            pltpu.VMEM((LANES, cells), f32),
            pltpu.VMEM((2,) + turned, f32),
            pltpu.VMEM((LANES, cells), f32),
            pltpu.VMEM((2, groups, 4 * devices, LANES), f32),
            pltpu.VMEM((8, -(-rows // LANES) * LANES), f32),
            pltpu.VMEM((rows_a, LANES), f32),
            pltpu.VMEM((rows_b, LANES), f32),
            pltpu.VMEM((rows_c, cells), f32),
            pltpu.VMEM((16, LANES), f32),
            pltpu.VMEM((peers, rows_a, LANES), f32),
            pltpu.VMEM((peers, rows_b, LANES), f32),
            pltpu.VMEM((rows_c, cells), f32),
            pltpu.VMEM((peers, 16, LANES), f32),
            pltpu.SemaphoreType.DMA((4,)),
            pltpu.SemaphoreType.DMA((2,)),
            pltpu.SemaphoreType.DMA((2,)),
            pltpu.SemaphoreType.DMA((4, 2)),
        ],
        compiler_params=pltpu.CompilerParams(
            collective_id=0, has_side_effects=True, vmem_limit_bytes=40 * 1024 * 1024
        ),
        name="implicit_lines",
    )(
        pltpu.with_memory_space_constraint(velocity.reshape(slabs, rows, cells), pltpu.HBM),
        pltpu.with_memory_space_constraint(viscosity.reshape(lines, cells), pltpu.HBM),
        pltpu.with_memory_space_constraint(y_coef, pltpu.HBM),
    )
    return result.reshape(velocity.shape)


def solution(mesh):
    placed = (P(None, None, "wall", "stream"), P(None, "wall", "stream"), P(None, "wall"))
    return jax.shard_map(
        functools.partial(shards, mesh.shape["stream"], mesh.shape["wall"]),
        mesh=mesh,
        in_specs=placed,
        out_specs=P(None, None, "wall", "stream"),
        check_vma=False,
    )
```

```python
import functools

import jax
import jax.numpy as jnp
from jax import lax
from jax.experimental import pallas as pl
from jax.experimental.pallas import tpu as pltpu
from jax.sharding import PartitionSpec as P

SEGMENTS = 8
PIECES = 2
LANES = 128
MESH = pl.DeviceIdType.MESH


def up8(rows):
    return -(-rows // 8) * 8


def join_matrix(a, b, link):
    a00, a0l, all_ = a
    b00, b0l, bll = b
    gain = link / (1.0 + link * (all_ + b00))
    left = gain * a0l
    right = gain * b0l
    return (a00 - left * a0l, left * b0l, bll - right * b0l), (gain, left, right)


def join_values(a, b, weights):
    _, left, right = weights
    jump = [al - b0 for al, b0 in zip(a[1], b[0])]
    first = [a0 - left * j for a0, j in zip(a[0], jump)]
    last = [bl + right * j for bl, j in zip(b[1], jump)]
    return (first, last), jump


def join_tree(blocks):
    levels = []
    while len(blocks) > 1:
        merged, weights = [], []
        for i in range(0, len(blocks) - 1, 2):
            (ma, fa, la), (mb, fb, lb) = blocks[i], blocks[i + 1]
            m, w = join_matrix(ma, mb, 0.5 * (la + fb))
            merged.append((m, fa, lb))
            weights.append(w)
        if len(blocks) % 2:
            merged.append(blocks[-1])
        levels.append(weights)
        blocks = merged
    return blocks[0], levels


def value_tree(values, levels):
    jumps = []
    for weights in levels:
        merged, jump = [], []
        for i, w in enumerate(weights):
            v, j = join_values(values[2 * i], values[2 * i + 1], w)
            merged.append(v)
            jump.append(j)
        if len(values) % 2:
            merged.append(values[-1])
        jumps.append(jump)
        values = merged
    return values[0], jumps


def down_tree(levels, jumps, inflow, outflow):
    flows = [(inflow, outflow)]
    for depth in reversed(range(len(levels))):
        spread = []
        for i, (gain, left, right) in enumerate(levels[depth]):
            fin, fout = flows[i]
            middle = None
            for term, weight in ((fin, left), (fout, right)):
                if term is not None:
                    part = weight if isinstance(term, float) else term * weight
                    middle = part if middle is None else middle + part
            if jumps is not None:
                part = gain * jumps[depth][i]
                middle = part if middle is None else middle + part
            spread += [(fin, middle), (middle, fout)]
        flows = spread + flows[len(levels[depth]) :]
    return flows


def odd(rows):
    return rows | 1


def total(terms):
    result = None
    for term in terms:
        if term is not None:
            result = term if result is None else result + term
    return result


def times(weight, flow):
    return None if flow is None else weight if isinstance(flow, float) else weight * flow


def kernel(devices, wall_devices, planes, vel_hbm, visc_hbm, coef_hbm, out,
           vel, visc, coef, edge, wall_out, got_w, got_s, stiff_t, src, src_t, ratio_s, inv_s, head_s, y_s, seg_a, seg_b,
           seg_f, flow, sol_t, sol, rim, rim_t, rim_sol, weigh, coef_s, msg_a, msg_b, msg_c, msg_d, got_a, got_b, got_c, got_d,
           load_sem, wall_send, wall_recv, ring_sem):
    slabs, rows, cells = vel_hbm.shape
    components = slabs // planes
    lines = planes * rows
    groups = lines // LANES
    length = cells // SEGMENTS
    piece = length // PIECES
    pitch = odd(length)
    step = odd(groups)
    me = lax.axis_index("stream")
    wall = lax.axis_index("wall")
    has_below = wall > 0
    has_above = wall < wall_devices - 1
    second = lax.rem(me, 2)
    is_first, is_second = second == 0, second == 1
    barrier = pltpu.get_barrier_semaphore()
    edges = [
        pltpu.make_async_copy(vel_hbm.at[:, rows - 8 : rows, :], edge.at[0], load_sem.at[3]),
        pltpu.make_async_copy(vel_hbm.at[:, 0:8, :], edge.at[1], load_sem.at[3]),
    ]
    loads = [
        pltpu.make_async_copy(visc_hbm, visc, load_sem.at[0]),
        pltpu.make_async_copy(coef_hbm, coef, load_sem.at[1]),
    ] + [
        pltpu.make_async_copy(
            vel_hbm.at[:, :, h * LANES : (h + 1) * LANES], vel.at[h, :, 8 : 8 + rows, :], load_sem.at[2])
        for h in range(cells // LANES)
    ]
    def await_all(landed, sem):
        pltpu.make_async_copy(landed, landed, sem).wait()

    def around(d):
        return lax.rem(me + d, devices)

    def greet(target):
        pl.semaphore_signal(barrier, inc=1, device_id={"wall": target}, device_id_type=MESH)

        @pl.when(is_second)
        def _():
            pl.semaphore_signal(
                barrier, inc=1, device_id={"wall": target, "stream": me - 1}, device_id_type=MESH)

    got_d[...] = jnp.zeros(got_d.shape, jnp.float32)
    msg_d[...] = jnp.zeros(msg_d.shape, jnp.float32)

    @pl.when(has_below)
    def _():
        greet(wall - 1)

    @pl.when(has_above)
    def _():
        greet(wall + 1)

    for d in sorted(range(1, devices), key=lambda d: -min(d, devices - d)):
        pl.semaphore_signal(barrier, inc=1, device_id={"stream": around(d)}, device_id_type=MESH)

    for load in edges + loads:
        load.start()

    nothing = jnp.zeros((cells // LANES, slabs, 1, LANES), jnp.float32)
    vel[:, :, 7:8, :] = nothing
    vel[:, :, 8 + rows : 9 + rows, :] = nothing
    wall_out[...] = jnp.zeros(wall_out.shape, jnp.float32)
    await_all(edge, load_sem.at[3])
    for a in range(slabs):
        wall_out[0, a : a + 1, :] = edge[0, a, 7:8, :]
        wall_out[1, a : a + 1, :] = edge[1, a, 0:1, :]

    def wall_copy(side, target):
        return pltpu.make_async_remote_copy(
            src_ref=wall_out.at[side], dst_ref=got_w.at[side],
            send_sem=wall_send.at[side], recv_sem=wall_recv.at[side],
            device_id={"wall": target}, device_id_type=MESH)

    def beside_copy(side, target):
        return pltpu.make_async_remote_copy(
            src_ref=wall_out.at[side], dst_ref=got_s.at[side],
            send_sem=wall_send.at[side], recv_sem=wall_recv.at[side],
            device_id={"wall": target, "stream": me + 1 - 2 * second}, device_id_type=MESH)

    rows_copy = pltpu.make_async_remote_copy(
        src_ref=msg_c, dst_ref=got_c, send_sem=ring_sem.at[2, 0], recv_sem=ring_sem.at[2, 1],
        device_id={"stream": me + 1 - 2 * second}, device_id_type=MESH)

    def ring_copy(d, source, target, send, recv):
        return pltpu.make_async_remote_copy(
            src_ref=source, dst_ref=target.at[d - 1],
            send_sem=send, recv_sem=recv,
            device_id={"stream": around(d)}, device_id_type=MESH)

    def at_position(i):
        return pl.ds(i, SEGMENTS, stride=pitch)

    def put_segments(buffer, slot, value):
        for g in range(groups):
            buffer[slot, pl.ds(g, SEGMENTS, stride=step), :] = value[g]

    def take_segment(buffer, slot, s):
        return buffer[slot, s * step : s * step + groups, :]

    def spread_rows(target, turned):
        for s in range(SEGMENTS):
            target[s * pitch : s * pitch + length, :] = turned[s * length : (s + 1) * length, :]

    def gather_rows(source):
        return jnp.concatenate([source[s * pitch : s * pitch + length, :] for s in range(SEGMENTS)])

    def factor(source, g):
        one = jnp.ones((SEGMENTS, LANES), jnp.float32)
        excess, reach = [one] * PIECES, [one] * PIECES
        corner = [None] * PIECES
        stiff = [source[at_position(b * piece), :] for b in range(PIECES)]
        starts = list(stiff)
        blocks = []
        for t in range(piece):
            for b in range(PIECES):
                i = b * piece + t
                if t < piece - 1:
                    following = source[at_position(i + 1), :]
                    link = 0.5 * (stiff[b] + following)
                    stiff[b] = following
                    inv = 1.0 / (excess[b] + link)
                    ratio = link * inv
                    ratio_s[i, g] = ratio
                else:
                    inv = 1.0 / excess[b]
                head = reach[b] * inv
                inv_s[i, g] = inv
                head_s[i, g] = head
                corner[b] = head * reach[b] if t == 0 else corner[b] + head * reach[b]
                if t < piece - 1:
                    excess[b] = 1.0 + ratio * excess[b]
                    reach[b] = reach[b] * ratio
                else:
                    blocks.append(((corner[b], head, inv), starts[b], stiff[b]))
        return blocks

    def forward(load, keep, g, fields):
        y = [[None] * fields for _ in range(PIECES)]
        first = [[None] * fields for _ in range(PIECES)]
        final = [[None] * fields for _ in range(PIECES)]
        for t in range(piece):
            for b in range(PIECES):
                i = b * piece + t
                head = head_s[i, g]
                ratio = ratio_s[i - 1, g] if t else None
                for c in range(fields):
                    f = load(c, i)
                    y[b][c] = f + ratio * y[b][c] if t else f
                    keep(c, i, y[b][c])
                    first[b][c] = first[b][c] + head * y[b][c] if t else head * y[b][c]
                    if t == piece - 1:
                        final[b][c] = inv_s[i, g] * y[b][c]
        return first, final

    def backward(spread, kept, put, g):
        for b in range(PIECES):
            now = [None] * len(spread)
            for t in reversed(range(piece)):
                i = b * piece + t
                head = head_s[i, g]
                inv = inv_s[i, g]
                if t < piece - 1:
                    ratio = ratio_s[i, g]
                for f in range(len(spread)):
                    fin, fout = spread[f][b]
                    terms = [times(head, fin)]
                    if kept is not None:
                        terms.append(kept(f, i) * inv)
                    if t < piece - 1:
                        terms.append(ratio * now[f])
                    value = total(terms)
                    if t == piece - 1 and fout is not None:
                        value = value - fout * inv
                    now[f] = value
                    put(f, i, value)

    loads[0].wait()
    parts = []
    for g in range(groups):
        spread_rows(stiff_t.at[g], visc[g * LANES : (g + 1) * LANES, :].T)
        parts.append(factor(stiff_t.at[g], g))
    blocks = [
        (tuple(jnp.stack([p[b][0][q] for p in parts]) for q in range(3)),
         jnp.stack([p[b][1] for p in parts]), jnp.stack([p[b][2] for p in parts]))
        for b in range(PIECES)
    ]
    whole, piece_levels = join_tree(blocks)
    for slot, value in enumerate(whole[0] + whole[1:]):
        put_segments(seg_a, slot, value)
    blocks = []
    for s in range(SEGMENTS):
        v = [take_segment(seg_a, slot, s) for slot in range(5)]
        blocks.append((tuple(v[:3]), v[3], v[4]))
    mine, levels = join_tree(blocks)
    for q, value in enumerate(mine[0] + (mine[1], mine[2])):
        msg_a[q * groups : (q + 1) * groups, :] = value

    each = 2 - second
    beside = jnp.where(has_below, each, 0) + jnp.where(has_above, each, 0)
    pl.semaphore_wait(barrier, devices - 1 + beside)

    def send_rows(side, target):
        @pl.when(is_first)
        def _():
            beside_copy(side, target).start()

        wall_copy(side, target).start()

    @pl.when(has_below)
    def _():
        send_rows(1, wall - 1)

    @pl.when(has_above)
    def _():
        send_rows(0, wall + 1)

    @pl.when(jnp.logical_not(has_below))
    def _():
        got_w[0] = jnp.zeros(got_w.shape[1:], jnp.float32)
        got_s[0] = jnp.zeros(got_w.shape[1:], jnp.float32)

    @pl.when(jnp.logical_not(has_above))
    def _():
        got_w[1] = jnp.zeros(got_w.shape[1:], jnp.float32)
        got_s[1] = jnp.zeros(got_w.shape[1:], jnp.float32)

    for d in range(1, devices):
        ring_copy(d, msg_a, got_a, ring_sem.at[0, 0], ring_sem.at[0, 1]).start()
    zero = jnp.zeros((groups, LANES), jnp.float32)
    unit = jnp.ones((groups, LANES), jnp.float32)

    def solve_fields(chosen):
        for f in chosen:
            if f < components:
                picked = [[j[f] for j in level] for level in jumps]
                flows = down_tree(levels, picked, None, None)
            elif f == components:
                flows = down_tree(levels, None, 1.0, None)
            else:
                flows = down_tree(levels, None, None, 1.0)
            for s, (fin, fout) in enumerate(flows):
                for side, term in enumerate((fin, fout)):
                    term = zero if term is None else unit if isinstance(term, float) else term
                    seg_f[2 * f + side, s * step : s * step + groups, :] = term
        for g in range(groups):
            near = [[tuple(w[g] for w in weights) for weights in level] for level in piece_levels]
            spread = []
            for f in chosen:
                fin, fout = (seg_f[2 * f + side, pl.ds(g, SEGMENTS, stride=step), :] for side in range(2))
                picked = [[j[f][g] for j in level] for level in piece_jumps] if f < components else None
                spread.append(down_tree(near, picked, fin, fout))

            def put(n, i, value, g=g):
                sol_t[chosen[n], g, at_position(i), :] = value

            kept = None if chosen[0] >= components else lambda n, i, g=g: y_s[chosen[n], i, g]
            backward(spread, kept, put, g)
            for f in chosen:
                sol[f, g * LANES : (g + 1) * LANES, :] = gather_rows(sol_t.at[f, g]).T

    solve_fields([components, components + 1])
    ends = [(side, p, p * rows + side * (rows - 1)) for side in range(2) for p in range(planes)]
    for side, p, r in ends:
        for f in range(2):
            e = (f * 2 + side) * planes + p
            msg_c[e : e + 1, :] = sol[components + f, r : r + 1, :]
    @pl.when(is_first)
    def _():
        rows_copy.start()

    row_plane = lax.broadcasted_iota(jnp.int32, (8, 1), 0) % planes

    def by_plane(pick):
        tile = pick(0)
        for p in range(1, planes):
            tile = jnp.where(row_plane == p, pick(p), tile)
        return tile

    def side_rows(source, f, side):
        base = (f * 2 + side) * planes
        return by_plane(lambda p: source[base + p : base + p + 1, :])
    loads[1].wait()
    coef_s[...] = jnp.zeros(coef_s.shape, jnp.float32)
    coef_s[0:2, 0:rows] = coef[...]
    slopes = coef_s[...].T
    await_all(vel.at[:, :, 8 : 8 + rows, :], load_sem.at[2])
    for r in range(0, rows, 8):
        up = jnp.broadcast_to(slopes[r : r + 8, 0:1], (8, LANES))
        down = jnp.broadcast_to(slopes[r : r + 8, 1:2], (8, LANES))
        keep = 1.0 - up - down
        for a in range(slabs):
            c, p = a // planes, a % planes
            for h in range(cells // LANES):
                src[c, p * rows + r : p * rows + r + 8, h * LANES : (h + 1) * LANES] = (
                    keep * vel[h, a, 8 + r : 16 + r, :]
                    + up * vel[h, a, 9 + r : 17 + r, :]
                    + down * vel[h, a, 7 + r : 15 + r, :]
                )
    firsts, finals = [], []
    for g in range(groups):
        for c in range(components):
            spread_rows(src_t.at[c, g], src[c, g * LANES : (g + 1) * LANES, :].T)

        def keep_y(c, i, value, g=g):
            y_s[c, i, g] = value

        first, final = forward(lambda c, i, g=g: src_t[c, g, at_position(i), :], keep_y, g, components)
        firsts.append(first)
        finals.append(final)
    values = [
        ([jnp.stack([v[b][c] for v in firsts]) for c in range(components)],
         [jnp.stack([v[b][c] for v in finals]) for c in range(components)])
        for b in range(PIECES)
    ]
    whole, piece_jumps = value_tree(values, piece_levels)
    for slot, value in enumerate(whole[0] + whole[1]):
        put_segments(seg_b, slot, value)
    values = []
    for s in range(SEGMENTS):
        v = [take_segment(seg_b, slot, s) for slot in range(2 * components)]
        values.append((v[:components], v[components:]))
    own, jumps = value_tree(values, levels)
    for q, value in enumerate(own[0] + own[1]):
        msg_b[q * groups : (q + 1) * groups, :] = value
    for d in range(1, devices):
        ring_copy(d, msg_b, got_b, ring_sem.at[1, 0], ring_sem.at[1, 1]).start()
    @pl.when(is_second)
    def _():
        rows_copy.wait_recv()

        @pl.when(has_below)
        def _():
            await_all(got_w, wall_recv.at[0])

        @pl.when(has_above)
        def _():
            await_all(got_w, wall_recv.at[1])

        lane_kind = lax.broadcasted_iota(jnp.int32, (8, LANES), 1) % 4
        for side in range(2):
            tile = None
            for n, (halo, source) in enumerate(((got_w, msg_c), (got_s, got_c))):
                for f in range(2):
                    value = jnp.sum(halo[side] * side_rows(source, f, side), axis=1, keepdims=True)
                    value = jnp.broadcast_to(value, (8, LANES))
                    tile = value if tile is None else jnp.where(lane_kind == 2 * n + f, value, tile)
            msg_d[side * 8 : side * 8 + 8, :] = tile
        for d in range(1, devices):
            ring_copy(d, msg_d, got_d, ring_sem.at[3, 0], ring_sem.at[3, 1]).start()
    solve_fields(list(range(components)))
    rim[...] = jnp.ones(rim.shape, jnp.float32)
    for side, p, r in ends:
        for c in range(components):
            e = side * 8 + c * planes + p
            rim[e : e + 1, :] = visc[r : r + 1, :]
    spread_rows(rim_t.at[0], rim[...].T)
    whole, rim_piece_levels = join_tree(factor(rim_t.at[0], groups))
    rim_blocks = whole[0] + whole[1:]
    for slot, value in enumerate(rim_blocks):
        seg_a[slot, 0:SEGMENTS, :] = value
    blocks = []
    for s in range(SEGMENTS):
        v = [seg_a[slot, s : s + 1, :] for slot in range(5)]
        blocks.append((tuple(v[:3]), v[3], v[4]))
    _, rim_levels = join_tree(blocks)

    scales = (slopes[0:1, 1:2], slopes[rows - 1 : rows, 0:1])
    await_all(got_a, ring_sem.at[0, 1])
    others = []
    for t in range(1, devices):
        slot = devices - t - 1
        v = [got_a[slot, q * groups : (q + 1) * groups, :] for q in range(5)]
        others.append((tuple(v[:3]), v[3], v[4]))
    rest, ring_levels = join_tree(others)
    (m00, m0l, mll), m_first, m_last = mine
    (b00, b0l, bll), b_first, b_last = rest
    out_diag = 2.0 / (m_last + b_first) + mll + b00
    in_diag = 2.0 / (b_last + m_first) + bll + m00
    cross = m0l + b0l
    det = 1.0 / (out_diag * in_diag - cross * cross)
    near_in, near_out, across = out_diag * det, in_diag * det, cross * det

    def put_weights(leaf, weights):
        for way in range(2):
            for f in range(2):
                for n in range(2):
                    k = 4 * ((leaf - n) % devices) + 2 * n + f
                    for g in range(groups):
                        weigh[way, g, k : k + 1, :] = weights[way][f][g : g + 1]

    put_weights(0, ((0.0 - near_in, 0.0 - across), (0.0 - across, 0.0 - near_out)))
    to_first = down_tree(ring_levels, None, 1.0, None)
    to_last = down_tree(ring_levels, None, None, 1.0)
    for t in range(1, devices):
        pairs = list(zip(to_first[t - 1], to_last[t - 1]))
        put_weights(devices - t, [
            [0.0 - total((times(by_first, from_first), times(by_last, from_last))) for from_first, from_last in pairs]
            for by_first, by_last in ((across, near_in), (near_out, across))
        ])
    tables = {}
    for way in range(2):
        turned = [weigh[way, g].T for g in range(groups)]
        for side in range(2):
            def pick(p):
                r = p * rows + side * (rows - 1)
                line = r % LANES
                return turned[r // LANES][line : line + 1, :]
            tables[side, way] = by_plane(pick) * scales[side]

    @pl.when(jnp.logical_and(is_first, has_below))
    def _():
        wall_copy(0, wall).wait_recv()

    @pl.when(jnp.logical_and(is_first, has_above))
    def _():
        wall_copy(1, wall).wait_recv()

    for side in range(2):
        rim[side * 8 : side * 8 + 8, :] = got_w[side] * scales[side]
    spread_rows(rim_t.at[0], rim[...].T)
    held = {}

    def keep_rim(c, i, value):
        held[i] = value

    first, final = forward(lambda c, i: rim_t[0, at_position(i), :], keep_rim, groups, 1)
    whole, rim_piece_jumps = value_tree([(first[b], final[b]) for b in range(PIECES)], rim_piece_levels)
    seg_b[0, 0:SEGMENTS, :] = whole[0][0]
    seg_b[1, 0:SEGMENTS, :] = whole[1][0]
    _, rim_jumps = value_tree(
        [([seg_b[0, s : s + 1, :]], [seg_b[1, s : s + 1, :]]) for s in range(SEGMENTS)], rim_levels)
    picked = [[j[0] for j in level] for level in rim_jumps]
    for s, terms in enumerate(down_tree(rim_levels, picked, None, None)):
        for side, term in enumerate(terms):
            term = jnp.zeros((1, LANES), jnp.float32) if term is None else term
            seg_f[side, s : s + 1, :] = term
    picked = [[j[0] for j in level] for level in rim_piece_jumps]
    spread = [down_tree(rim_piece_levels, picked, seg_f[0, 0:SEGMENTS, :], seg_f[1, 0:SEGMENTS, :])]

    def put_rim(n, i, value):
        rim_t[1, at_position(i), :] = value

    backward(spread, lambda n, i: held[i], put_rim, groups)
    rim_sol[...] = gather_rows(rim_t.at[1]).T
    await_all(got_b, ring_sem.at[1, 1])
    theirs = []
    for t in range(1, devices):
        slot = devices - t - 1
        v = [got_b[slot, q * groups : (q + 1) * groups, :] for q in range(2 * components)]
        theirs.append((v[:components], v[components:]))
    tail, _ = value_tree(theirs, ring_levels)
    for c in range(components):
        gap_out = own[1][c] - tail[0][c]
        gap_in = tail[1][c] - own[0][c]
        outflow = near_out * gap_out + across * gap_in
        inflow = near_in * gap_in + across * gap_out
        for g in range(groups):
            flow[g, c : c + 1, :] = inflow[g : g + 1]
            flow[g, components + c : components + c + 1, :] = outflow[g : g + 1]

    for g in range(groups):
        span = slice(g * LANES, (g + 1) * LANES)
        columns = flow[g].T
        from_left = sol[components, span, :]
        from_right = sol[components + 1, span, :]
        for c in range(components):
            out[c, span, :] = (
                sol[c, span, :]
                + columns[:, c : c + 1] * from_left
                + columns[:, components + c : components + c + 1] * from_right
            )
    for n, sent in enumerate((got_a, got_b)):
        await_all(sent, ring_sem.at[n, 0])

    @pl.when(is_first)
    def _():
        rows_copy.wait_send()

        @pl.when(has_above)
        def _():
            await_all(got_w, wall_send.at[0])

        @pl.when(has_below)
        def _():
            await_all(got_w, wall_send.at[1])

        await_all(got_d.at[0 : devices // 2], ring_sem.at[3, 1])

    @pl.when(is_second)
    def _():
        @pl.when(has_above)
        def _():
            await_all(got_w.at[0], wall_send.at[0])

        @pl.when(has_below)
        def _():
            await_all(got_w.at[1], wall_send.at[1])

        await_all(got_d, ring_sem.at[3, 0])
        await_all(got_d.at[0 : devices // 2 - 1], ring_sem.at[3, 1])

    lane_slot = lax.broadcasted_iota(jnp.int32, (8, 4 * devices), 1) // 4
    for side in range(2):
        held_rows = slice(side * 8, side * 8 + 8)
        mix = jnp.where(is_second, msg_d[held_rows, 0 : 4 * devices], 0.0)
        for d in range(1, devices):
            mix = jnp.where(lane_slot == d, got_d[d - 1, held_rows, 0 : 4 * devices], mix)
        ways = [jnp.sum(mix * tables[side, way], axis=1, keepdims=True) for way in range(2)]
        added = (
            rim_sol[side * 8 : side * 8 + 8, :] + ways[0] * side_rows(msg_c, 0, side) + ways[1] * side_rows(msg_c, 1, side)
        )
        for c in range(components):
            for p in range(planes):
                r = p * rows + side * (rows - 1)
                e = c * planes + p
                out[c, r : r + 1, :] = out[c, r : r + 1, :] + added[e : e + 1, :]


def shards(devices, wall_devices, velocity, viscosity, y_coef):
    components, planes, rows, cells = velocity.shape
    lines = planes * rows
    slabs = components * planes
    groups = lines // LANES
    length = cells // SEGMENTS
    fields = components + 2
    f32 = jnp.float32
    rows_a, rows_b, rows_c = up8(5 * groups), up8(2 * components * groups), up8(4 * planes)
    peers = devices - 1
    sweeps = (length, groups + 1, SEGMENTS, LANES)
    turned = (SEGMENTS * odd(length), LANES)
    joints = SEGMENTS * odd(groups)
    vmem = pl.BlockSpec(memory_space=pltpu.VMEM)
    result = pl.pallas_call(
        functools.partial(kernel, devices, wall_devices, planes),
        out_shape=jax.ShapeDtypeStruct((components, lines, cells), f32),
        in_specs=[pl.BlockSpec(memory_space=pltpu.HBM)] * 3,
        out_specs=vmem,
        scratch_shapes=[
            pltpu.VMEM((cells // LANES, slabs, rows + 16, LANES), f32),
            pltpu.VMEM((lines, cells), f32),
            pltpu.VMEM(y_coef.shape, f32),
            pltpu.VMEM((2, slabs, 8, cells), f32),
            pltpu.VMEM((2, 8, cells), f32),
            pltpu.VMEM((2, 8, cells), f32),
            pltpu.VMEM((2, 8, cells), f32),
            pltpu.VMEM((groups,) + turned, f32),
            pltpu.VMEM((components, lines, cells), f32),
            pltpu.VMEM((components, groups) + turned, f32),
            pltpu.VMEM(sweeps, f32),
            pltpu.VMEM(sweeps, f32),
            pltpu.VMEM(sweeps, f32),
            pltpu.VMEM((components, length, groups, SEGMENTS, LANES), f32),
            pltpu.VMEM((5, joints, LANES), f32),
            pltpu.VMEM((2 * components, joints, LANES), f32),
            pltpu.VMEM((2 * fields, joints, LANES), f32),
            pltpu.VMEM((groups, up8(2 * components), LANES), f32),
            pltpu.VMEM((fields, groups) + turned, f32),
            pltpu.VMEM((fields, lines, cells), f32),
            pltpu.VMEM((LANES, cells), f32),
            pltpu.VMEM((2,) + turned, f32),
            pltpu.VMEM((LANES, cells), f32),
            pltpu.VMEM((2, groups, 4 * devices, LANES), f32),
            pltpu.VMEM((8, -(-rows // LANES) * LANES), f32),
            pltpu.VMEM((rows_a, LANES), f32),
            pltpu.VMEM((rows_b, LANES), f32),
            pltpu.VMEM((rows_c, cells), f32),
            pltpu.VMEM((16, LANES), f32),
            pltpu.VMEM((peers, rows_a, LANES), f32),
            pltpu.VMEM((peers, rows_b, LANES), f32),
            pltpu.VMEM((rows_c, cells), f32),
            pltpu.VMEM((peers, 16, LANES), f32),
            pltpu.SemaphoreType.DMA((4,)),
            pltpu.SemaphoreType.DMA((2,)),
            pltpu.SemaphoreType.DMA((2,)),
            pltpu.SemaphoreType.DMA((4, 2)),
        ],
        compiler_params=pltpu.CompilerParams(
            collective_id=0, has_side_effects=True, vmem_limit_bytes=40 * 1024 * 1024
        ),
        name="implicit_lines",
    )(
        pltpu.with_memory_space_constraint(velocity.reshape(slabs, rows, cells), pltpu.HBM),
        pltpu.with_memory_space_constraint(viscosity.reshape(lines, cells), pltpu.HBM),
        pltpu.with_memory_space_constraint(y_coef, pltpu.HBM),
    )
    return result.reshape(velocity.shape)


def solution(mesh):
    placed = (P(None, None, "wall", "stream"), P(None, "wall", "stream"), P(None, "wall"))
    return jax.shard_map(
        functools.partial(shards, mesh.shape["stream"], mesh.shape["wall"]),
        mesh=mesh,
        in_specs=placed,
        out_specs=P(None, None, "wall", "stream"),
        check_vma=False,
    )
```
